1024 devices in a mesh: seq: 64 (over x, y, core), chan: 16 (over z).
Axes of the slice: x: 4, y: 8, z: 16, core: 2. Of those that a mesh axis runs over, the one named last changes fastest.
Arguments:
- hyena_query: float32 [8192, 8192], P('chan', 'seq'), may hold values from -6 to 6
- hyena_key: float32 [8192, 8192], P('chan', 'seq'), may hold values from -6 to 6
- hyena_value: float32 [8192, 8192], P('chan', 'seq'), may hold values from -6 to 6
- long_filter: float32 [8192, 8192], P('chan', 'seq'), may hold values from -1.1 to 1.1
- queries: float32 [8192, 8192], P('seq', 'chan'), may hold values from -10 to 10
- keys: float32 [8192, 8192], P('seq', 'chan'), may hold values from -10 to 10
- key_blocks: int32 [64, 4], P('seq'), may hold values from -1 to 63, as said below
Outputs:
- hyena_out: float32 [8192, 8192], P('chan', 'seq')
- attended: float32 [8192, 8192], P('seq', 'chan')
The draws below stay inside these ranges and needn't reach their ends.
Inputs may be any that keep to these rules, and one draw needn't show every extreme that they name: `key_blocks`: row i lists block i itself and up to 3 distinct other blocks among i - 3 .. i - 1, in any order; unused entries are -1. How many blocks a row lists varies from row to row, and some row lists 4.
All inputs are finite; a program needn't handle non-finite values.
Results may differ from the reference program's by a relative error of at most 0.0003.
Values sent between devices are 32-bit elements; how exact they have to be, the bound alone decides.
A program may use at most 32 MiB of HBM per device.

```python
import math
import jax
import jax.numpy as jnp
from jax import lax

FILTER_CHANNELS = 8192
HEADS = 64
HEAD_DIM = 128
L_DEV = 128
WIN = 4
SEQUENCE_TOKENS = 8192
BLOCKS = 64
N_CHAN = 16


def draw_long_filter(key, part):
    token_positions = jnp.arange(SEQUENCE_TOKENS, dtype=jnp.float32)[None, :]
    share = 50
    slow = jax.random.randint(jax.random.fold_in(key, 21), (FILTER_CHANNELS, 1), 0, 100) < share
    slow_total = jnp.exp(jax.random.uniform(jax.random.fold_in(key, 22), (FILTER_CHANNELS, 1), minval=math.log(0.05), maxval=math.log(2.0)))
    slow_rate = slow_total / SEQUENCE_TOKENS
    fast_rate = jnp.exp(jax.random.uniform(jax.random.fold_in(key, 23), (FILTER_CHANNELS, 1), minval=math.log(1.0 / 50.0), maxval=math.log(1.0 / 30.0)))
    rate = jnp.where(slow, slow_rate, fast_rate)
    energy = jnp.sqrt(2.0 * rate / (1.0 - jnp.exp(-2.0 * rate * SEQUENCE_TOKENS)))
    decay_profile = jnp.exp(-rate * token_positions)
    spike_position = jax.random.randint(jax.random.fold_in(key, 24), (FILTER_CHANNELS, 3), 0, SEQUENCE_TOKENS).astype(jnp.float32)
    spike_retained = jax.random.uniform(jax.random.fold_in(key, 25), (FILTER_CHANNELS, 3), minval=0.5, maxval=0.8)
    for selected_index in range(3):
        decay_profile = decay_profile * jnp.where(token_positions >= spike_position[:, selected_index:selected_index + 1], spike_retained[:, selected_index:selected_index + 1], 1.0)
    noise = jnp.clip(jax.random.normal(jax.random.fold_in(key, 26), (FILTER_CHANNELS, SEQUENCE_TOKENS)), -4.0, 4.0)
    late_width = max(SEQUENCE_TOKENS // 8, 1)
    late_start = jax.random.randint(jax.random.fold_in(key, 27), (FILTER_CHANNELS, 1), SEQUENCE_TOKENS // 4, SEQUENCE_TOKENS // 2 + 1).astype(jnp.float32)
    late_window = (token_positions >= late_start) & (token_positions < late_start + late_width)
    late_noise = jnp.clip(jax.random.normal(jax.random.fold_in(key, 28), (FILTER_CHANNELS, SEQUENCE_TOKENS)), -4.0, 4.0)
    late_part = jnp.where(late_window & jnp.logical_not(slow), 0.04 * late_noise, 0.0)
    return ((noise * decay_profile + late_part) * energy).astype(jnp.float32)


def draw_queries(key, part):
    base = jnp.clip(jax.random.normal(jax.random.fold_in(key, 1), (SEQUENCE_TOKENS, HEADS * HEAD_DIM)), -6.0, 6.0)
    return base.astype(jnp.float32)


def draw_keys(key, part):
    base = jnp.clip(jax.random.normal(jax.random.fold_in(key, 2), (SEQUENCE_TOKENS, HEADS * HEAD_DIM)), -6.0, 6.0)
    return base.astype(jnp.float32)


def draw_key_blocks(key, part):
    rows = jnp.arange(BLOCKS, dtype=jnp.int32)
    counts = jax.random.randint(jax.random.fold_in(key, 31), (BLOCKS,), 1, WIN + 1)
    fullest = jax.random.randint(jax.random.fold_in(key, 32), (), WIN - 1, BLOCKS)
    counts = jnp.where(rows == fullest, WIN, counts)
    scores = jax.random.randint(jax.random.fold_in(key, 33), (BLOCKS, WIN - 1), 0, 1 << 20) * WIN + jnp.arange(WIN - 1, dtype=jnp.int32)[None, :]
    offsets = jnp.argsort(scores, axis=1).astype(jnp.int32) + 1
    entries = rows[:, None] - offsets
    valid = (jnp.arange(WIN - 1, dtype=jnp.int32)[None, :] < counts[:, None] - 1) & (entries >= 0)
    others = jnp.where(valid, entries, -1)
    return jnp.concatenate([rows[:, None], others], axis=1).astype(jnp.int32)


def level_of(own_key, shape, pieces, low, top_value):
    gain = 1.0
    for axis_at, blocks in pieces:
        heights = jax.random.uniform(jax.random.fold_in(jax.random.fold_in(own_key, 6), axis_at), (blocks,), jnp.float32, low / len(pieces), top_value / len(pieces))
        gain = gain * jnp.repeat(jnp.exp(heights), shape[axis_at] // blocks).reshape((-1,) + (1,) * (len(shape) - 1 - axis_at))
    return gain


def scatter_about(key, dims, scale, reach, shards=(), kind=jnp.bfloat16):
    gain = level_of(key, dims, shards, -0.22, 0.18) if shards else 1.0
    drawn = jax.random.normal(key, dims, jnp.float32) * scale * gain
    return jnp.minimum(jnp.maximum(drawn, -reach), reach).astype(kind)


def setup_inputs(seed: int = 0) -> dict:
    arg_keys = jax.random.split(jax.random.key(seed), 8)
    hyena_query = scatter_about(arg_keys[0], (FILTER_CHANNELS, SEQUENCE_TOKENS), 1.0, 6.0, ((0, 16), (1, 64)), jnp.float32)
    hyena_key = scatter_about(arg_keys[1], (FILTER_CHANNELS, SEQUENCE_TOKENS), 1.0, 6.0, ((0, 16), (1, 64)), jnp.float32)
    hyena_value = scatter_about(arg_keys[2], (FILTER_CHANNELS, SEQUENCE_TOKENS), 1.0, 6.0, ((0, 16), (1, 64)), jnp.float32)
    long_filter = draw_long_filter(jax.random.fold_in(arg_keys[7], 71), 0)
    queries = draw_queries(jax.random.fold_in(arg_keys[7], 71), 0)
    keys = draw_keys(jax.random.fold_in(arg_keys[7], 71), 0)
    key_blocks = draw_key_blocks(jax.random.fold_in(arg_keys[7], 71), 0)
    return dict(hyena_query=hyena_query, hyena_key=hyena_key, hyena_value=hyena_value, long_filter=long_filter, queries=queries, keys=keys, key_blocks=key_blocks)


def long_convolution(hyena_key, hyena_value, long_filter):
    gated = hyena_key * hyena_value
    length = gated.shape[1]
    padded = 2 * length

    def one_group(pair):
        signal, filt = pair
        spectrum = jnp.fft.rfft(signal, n=padded, axis=1) * jnp.fft.rfft(filt, n=padded, axis=1)
        return jnp.fft.irfft(spectrum, n=padded, axis=1)[:, :length]

    shaped = (gated.reshape(N_CHAN, -1, length), long_filter.reshape(N_CHAN, -1, length))
    return lax.map(one_group, shaped).reshape(gated.shape)


def block_attention(queries, keys, values, key_blocks):
    scale = HEAD_DIM ** -0.5
    query_four = queries.reshape(BLOCKS, L_DEV, HEADS, HEAD_DIM)
    key_four = keys.reshape(BLOCKS, L_DEV, HEADS, HEAD_DIM)
    value_four = values.reshape(BLOCKS, L_DEV, HEADS, HEAD_DIM)
    token_positions = jnp.arange(L_DEV, dtype=jnp.int32)

    def one_block(index):
        listed = key_blocks[index]
        safe = jnp.maximum(listed, 0).astype(jnp.int32)
        key_rows = key_four[safe].reshape(WIN * L_DEV, HEADS, HEAD_DIM)
        value_rows = value_four[safe].reshape(WIN * L_DEV, HEADS, HEAD_DIM)
        allowed = (listed[:, None, None] >= 0) & ((listed[:, None, None] < index) | (token_positions[None, None, :] <= token_positions[None, :, None]))
        allowed = jnp.transpose(allowed, (1, 0, 2)).reshape(L_DEV, WIN * L_DEV)
        scores = jnp.einsum('qhd,khd->hqk', query_four[index], key_rows, precision=lax.Precision.HIGHEST) * scale
        scores = jnp.where(allowed[None], scores, -1e30)
        top = jnp.max(scores, axis=-1, keepdims=True)
        expo = jnp.exp(scores - top)
        weights = expo / jnp.sum(expo, axis=-1, keepdims=True)
        out = jnp.einsum('hqk,khd->qhd', weights, value_rows, precision=lax.Precision.HIGHEST)
        return out.reshape(L_DEV, HEADS * HEAD_DIM)

    return lax.map(one_block, jnp.arange(BLOCKS, dtype=jnp.int32)).reshape(queries.shape)


def reference(hyena_query, hyena_key, hyena_value, long_filter, queries, keys, key_blocks):
    convolved = long_convolution(hyena_key, hyena_value, long_filter)
    hyena_out = hyena_query * convolved
    values = jnp.transpose(hyena_out)
    attended = block_attention(queries, keys, values, key_blocks)
    return hyena_out, attended
```

```python
import functools

import jax
import jax.numpy as jnp
import numpy as np
from jax import lax
from jax.experimental import pallas as pl
from jax.experimental.pallas import tpu as pltpu
from jax.sharding import PartitionSpec as P

HEAD_DIM = 128
EXACT = lax.Precision.HIGHEST
CHANNELS = 8


def split(value):
    high = value.astype(jnp.bfloat16)
    low = (value - high.astype(jnp.float32)).astype(jnp.bfloat16)
    return high, low


def dot(left, right):
    return jnp.dot(left, right, preferred_element_type=jnp.float32)


def dot_nt(left, right, precision=None):
    return lax.dot_general(
        left,
        right,
        (((1,), (1,)), ((), ())),
        precision=precision,
        preferred_element_type=jnp.float32,
    )


def split_table(table):
    high = table.astype(np.float32).astype(jnp.bfloat16)
    low = (table - high.astype(np.float64)).astype(np.float32).astype(jnp.bfloat16)
    return high, low


def transform_tables(groups, length):
    total = 2 * groups * length
    half = np.arange(groups)[:, None] + 0.5
    first = 2 * np.pi * half * np.arange(groups)[None, :] / (2 * groups)
    twist = 2 * np.pi * half * np.arange(length)[None, :] / total
    last = 2 * np.pi * np.arange(length)[:, None] * np.arange(length)[None, :] / length
    ahead = np.concatenate([np.cos(first), -np.sin(first)], axis=0)
    back = ahead.T * (2.0 / total)
    ahead_high, ahead_low = split_table(ahead)
    back_high, back_low = split_table(back)
    cosine, sine = np.cos(last), np.sin(last)
    forward = np.block([[cosine, -sine], [sine, cosine]])
    inverse = np.block([[cosine, sine], [-sine, cosine]])
    return (
        np.concatenate([ahead_high, ahead_high, ahead_low], axis=1),
        np.concatenate([back_high, back_high, back_low], axis=1),
        np.stack([np.cos(twist), np.sin(twist)]).astype(np.float32),
        np.stack(split_table(forward)),
        np.stack(split_table(inverse)),
    )


def three_pass(high_ref, low_ref, table_ref):
    high = high_ref[...]
    return dot(high, table_ref[0]) + dot(low_ref[...], table_ref[0]) + dot(high, table_ref[1])


def to_spectrum(block, ahead, twist, forward, high_ref, low_ref):
    groups, length = twist.shape[1:]
    twist_cos, twist_sin = twist[0], twist[1]
    for pair in range(CHANNELS // 2):
        high, low = split(jnp.concatenate([block(2 * pair), block(2 * pair + 1)], axis=1))
        mixed = dot(ahead[...], jnp.concatenate([high, low, high], axis=0))
        for side in range(2):
            real = mixed[:groups, side * length : (side + 1) * length]
            imag = mixed[groups:, side * length : (side + 1) * length]
            turned = jnp.concatenate(
                [real * twist_cos + imag * twist_sin, imag * twist_cos - real * twist_sin], axis=1
            )
            high, low = split(turned)
            rows = pl.ds((2 * pair + side) * groups, groups)
            high_ref[rows, :] = high
            low_ref[rows, :] = low
    return three_pass(high_ref, low_ref, forward)


def multiply_back(spectrum, other, back, twist, inverse, high_ref, low_ref, store):
    groups, length = twist.shape[1:]
    real = spectrum[:, :length] * other[:, :length] - spectrum[:, length:] * other[:, length:]
    imag = spectrum[:, :length] * other[:, length:] + spectrum[:, length:] * other[:, :length]
    high_ref[...], low_ref[...] = split(jnp.concatenate([real, imag], axis=1))
    mixed = three_pass(high_ref, low_ref, inverse)
    twist_cos, twist_sin = twist[0], twist[1]

    def turned(channel):
        part = mixed[channel * groups : (channel + 1) * groups]
        real, imag = part[:, :length], part[:, length:]
        return jnp.concatenate(
            [real * twist_cos - imag * twist_sin, imag * twist_cos + real * twist_sin], axis=0
        )

    for pair in range(CHANNELS // 2):
        high, low = split(jnp.concatenate([turned(2 * pair), turned(2 * pair + 1)], axis=1))
        signal = dot(back[...], jnp.concatenate([high, low, high], axis=0))
        store(2 * pair, signal[:, :length])
        store(2 * pair + 1, signal[:, length:])


def convolve_kernel(received, ahead, back, twist, forward, inverse, result, high, low, spectrum):
    groups = twist.shape[1]

    def block(which):
        return lambda k: received[pl.ds(which * CHANNELS + k, groups, stride=2 * CHANNELS), :]

    def store(k, value):
        result[pl.ds(k, groups, stride=CHANNELS), :] = value

    spectrum[...] = to_spectrum(block(1), ahead, twist, forward, high, low)
    signal = to_spectrum(block(0), ahead, twist, forward, high, low)
    multiply_back(signal, spectrum[...], back, twist, inverse, high, low, store)


def allowed_keys(key_blocks, source, offset, length):
    listed = jnp.max((key_blocks == source).astype(jnp.float32), axis=1, keepdims=True)
    listed = jnp.where(source >= 0, listed, 0.0) > 0.5
    if offset:
        return jnp.broadcast_to(listed, (length, length))
    rows = lax.broadcasted_iota(jnp.int32, (length, length), 0)
    cols = lax.broadcasted_iota(jnp.int32, (length, length), 1)
    return jnp.broadcast_to(listed, (length, length)) & (cols <= rows)


def attend_kernel(queries, key_blocks, *refs):
    keys, values, result = refs[:4], refs[4:8], refs[8]
    length, width = queries.shape
    span = len(keys)
    me = lax.axis_index("seq")
    allowed = [allowed_keys(key_blocks[...], me - o, o, length) for o in range(span)]
    for head in range(width // HEAD_DIM):
        cols = slice(head * HEAD_DIM, (head + 1) * HEAD_DIM)
        query = queries[:, cols] * HEAD_DIM ** (-0.5)
        scores = [
            jnp.where(allowed[o], dot_nt(query, keys[o][:, cols], EXACT), -1e30) for o in range(span)
        ]
        top = functools.reduce(jnp.maximum, scores)
        top = jnp.max(top, axis=1, keepdims=True)
        expo = [jnp.exp(s - top) for s in scores]
        total = jnp.sum(functools.reduce(jnp.add, expo), axis=1, keepdims=True)
        high, low = split(jnp.concatenate(expo, axis=1))
        value_high, value_low = split(jnp.concatenate([values[o][cols, :] for o in range(span)], axis=1))
        out = dot_nt(high, value_high) + dot_nt(low, value_high) + dot_nt(high, value_low)
        result[:, cols] = out / total


def call(kernel, shape, scratch, operands):
    return pl.pallas_call(
        kernel,
        out_shape=jax.ShapeDtypeStruct(shape, jnp.float32),
        in_specs=[pl.BlockSpec(memory_space=pltpu.VMEM)] * len(operands),
        out_specs=pl.BlockSpec(memory_space=pltpu.VMEM),
        scratch_shapes=scratch,
    )(*operands)


def from_before(array, distance):
    size = lax.axis_size("seq")
    return lax.ppermute(array, "seq", [(i, i + distance) for i in range(size - distance)])


def body(hyena_query, hyena_key, hyena_value, long_filter, queries, keys, key_blocks):
    channels, length = hyena_key.shape
    groups = lax.axis_size("seq")
    span = key_blocks.shape[1]
    shape = (groups, CHANNELS, length)
    sent = jnp.concatenate(
        [(hyena_key * hyena_value).reshape(shape), long_filter.reshape(shape)], axis=1
    )
    received = lax.all_to_all(sent, "seq", split_axis=0, concat_axis=0, tiled=True)
    tables = [jnp.asarray(t) for t in transform_tables(groups, length)]
    rows = CHANNELS * groups
    convolved = call(
        convolve_kernel,
        (rows, length),
        [
            pltpu.VMEM((rows, 2 * length), jnp.bfloat16),
            pltpu.VMEM((rows, 2 * length), jnp.bfloat16),
            pltpu.VMEM((rows, 2 * length), jnp.float32),
        ],
        [received.reshape(2 * rows, length), *tables],
    )
    mixed = lax.all_to_all(
        convolved.reshape(shape), "seq", split_axis=0, concat_axis=0, tiled=True
    )
    hyena_out = hyena_query * mixed.reshape(channels, length)
    all_keys = [keys] + [from_before(keys, o) for o in range(1, span)]
    all_values = [hyena_out] + [from_before(hyena_out, o) for o in range(1, span)]
    attended = call(
        attend_kernel, queries.shape, [], [queries, key_blocks, *all_keys, *all_values]
    )
    return (hyena_out, attended)


def solution(mesh):
    placed = (
        P("chan", "seq"),
        P("chan", "seq"),
        P("chan", "seq"),
        P("chan", "seq"),
        P("seq", "chan"),
        P("seq", "chan"),
        P("seq", None),
    )
    return jax.shard_map(
        body,
        mesh=mesh,
        in_specs=placed,
        out_specs=(P("chan", "seq"), P("seq", "chan")),
        check_vma=False,
    )
```

```python
import functools

import jax
import jax.numpy as jnp
import numpy as np
from jax import lax
from jax.experimental import pallas as pl
from jax.experimental.pallas import tpu as pltpu
from jax.sharding import PartitionSpec as P

HEAD_DIM = 128
EXACT = lax.Precision.HIGHEST
CHANNELS = 8


def split(value):
    high = value.astype(jnp.bfloat16)
    low = (value - high.astype(jnp.float32)).astype(jnp.bfloat16)
    return high, low


def dot(left, right):
    return jnp.dot(left, right, preferred_element_type=jnp.float32)


def dot_nt(left, right, precision=None):
    return lax.dot_general(
        left,
        right,
        (((1,), (1,)), ((), ())),
        precision=precision,
        preferred_element_type=jnp.float32,
    )


def split_table(table):
    high = table.astype(np.float32).astype(jnp.bfloat16)
    low = (table - high.astype(np.float64)).astype(np.float32).astype(jnp.bfloat16)
    return high, low


def transform_tables(groups, length):
    total = 2 * groups * length
    half = np.arange(groups)[:, None] + 0.5
    first = 2 * np.pi * half * np.arange(groups)[None, :] / (2 * groups)
    twist = 2 * np.pi * half * np.arange(length)[None, :] / total
    last = 2 * np.pi * np.arange(length)[:, None] * np.arange(length)[None, :] / length
    ahead = np.concatenate([np.cos(first), -np.sin(first)], axis=0)
    back = ahead.T * (2.0 / total)
    ahead_high, ahead_low = split_table(ahead)
    back_high, back_low = split_table(back)
    cosine, sine = np.cos(last), np.sin(last)
    forward = np.block([[cosine, -sine], [sine, cosine]])
    inverse = np.block([[cosine, sine], [-sine, cosine]])
    return (
        np.concatenate([ahead_high, ahead_high, ahead_low], axis=1),
        np.concatenate([back_high, back_high, back_low], axis=1),
        np.stack([np.cos(twist), np.sin(twist)]).astype(np.float32),
        np.stack(split_table(forward)),
        np.stack(split_table(inverse)),
    )


def three_pass(high_ref, low_ref, table_ref):
    high = high_ref[...]
    return dot(high, table_ref[0]) + dot(low_ref[...], table_ref[0]) + dot(high, table_ref[1])


def to_spectrum(block, ahead, twist, forward, high_ref, low_ref):
    groups, length = twist.shape[1:]
    twist_cos, twist_sin = twist[0], twist[1]
    for pair in range(CHANNELS // 2):
        high, low = split(jnp.concatenate([block(2 * pair), block(2 * pair + 1)], axis=1))
        mixed = dot(ahead[...], jnp.concatenate([high, low, high], axis=0))
        for side in range(2):
            real = mixed[:groups, side * length : (side + 1) * length]
            imag = mixed[groups:, side * length : (side + 1) * length]
            turned = jnp.concatenate(
                [real * twist_cos + imag * twist_sin, imag * twist_cos - real * twist_sin], axis=1
            )
            high, low = split(turned)
            rows = pl.ds((2 * pair + side) * groups, groups)
            high_ref[rows, :] = high
            low_ref[rows, :] = low
    return three_pass(high_ref, low_ref, forward)


def multiply_back(spectrum, other, back, twist, inverse, high_ref, low_ref, store):
    groups, length = twist.shape[1:]
    real = spectrum[:, :length] * other[:, :length] - spectrum[:, length:] * other[:, length:]
    imag = spectrum[:, :length] * other[:, length:] + spectrum[:, length:] * other[:, :length]
    high_ref[...], low_ref[...] = split(jnp.concatenate([real, imag], axis=1))
    mixed = three_pass(high_ref, low_ref, inverse)
    twist_cos, twist_sin = twist[0], twist[1]

    def turned(channel):
        part = mixed[channel * groups : (channel + 1) * groups]
        real, imag = part[:, :length], part[:, length:]
        return jnp.concatenate(
            [real * twist_cos - imag * twist_sin, imag * twist_cos + real * twist_sin], axis=0
        )

    for pair in range(CHANNELS // 2):
        high, low = split(jnp.concatenate([turned(2 * pair), turned(2 * pair + 1)], axis=1))
        signal = dot(back[...], jnp.concatenate([high, low, high], axis=0))
        store(2 * pair, signal[:, :length])
        store(2 * pair + 1, signal[:, length:])


def allowed_keys(key_blocks, source, offset, length):
    listed = jnp.max((key_blocks == source).astype(jnp.float32), axis=1, keepdims=True)
    listed = jnp.where(source >= 0, listed, 0.0) > 0.5
    if offset:
        return jnp.broadcast_to(listed, (length, length))
    rows = lax.broadcasted_iota(jnp.int32, (length, length), 0)
    cols = lax.broadcasted_iota(jnp.int32, (length, length), 1)
    return jnp.broadcast_to(listed, (length, length)) & (cols <= rows)


MESH = pl.DeviceIdType.MESH
X, Y, CORES = 4, 8, 2
GROUPS = X * Y * CORES
WIDE = GROUPS // 4


def peer_of(me, turn):
    step = turn + turn // 58
    core, way = step % 2, (step // 2) % 2
    over, reach = (step // 4) % 4, (step // 16) % 4
    along = (1 - way) * (4 + reach) + way * (3 - reach)
    x, y = me // (Y * CORES), (me // CORES) % Y
    return ((x + over + 2) % X * Y + (y + along) % Y) * CORES + (me + core) % CORES


def to_all(source, target, me, send_sem, recv_sem):
    mine = pl.ds(pl.multiple_of(me * CHANNELS, CHANNELS), CHANNELS)

    def send(turn, carry):
        peer = peer_of(me, turn)
        rows = pl.ds(pl.multiple_of(peer * CHANNELS, CHANNELS), CHANNELS)
        pltpu.make_async_remote_copy(
            src_ref=source.at[rows, :],
            dst_ref=target.at[mine, :],
            send_sem=send_sem,
            recv_sem=recv_sem,
            device_id={"seq": peer},
            device_id_type=MESH,
        ).start()
        return carry

    lax.fori_loop(0, GROUPS - 1, send, 0)
    pltpu.make_async_copy(source.at[mine, :], target.at[mine, :], recv_sem).start()


def done(ref, sem):
    pltpu.make_async_copy(ref, ref, sem).wait()


def start_to(source, target, peer, send_sem, recv_sem):
    pltpu.make_async_remote_copy(
        src_ref=source,
        dst_ref=target,
        send_sem=send_sem,
        recv_sem=recv_sem,
        device_id={"seq": peer},
        device_id_type=MESH,
    ).start()


def kernel(
    query_hbm, key_hbm, value_hbm, filter_hbm, queries_hbm, keys_hbm, key_blocks,
    ahead, back, twist, forward, inverse,
    hyena, attended,
    gate, gate_key, gate_value, taps, queries, keys, got_taps, got_gate, convolved, got_back,
    values, high, low, spectrum, weight_high, weight_low,
    load_sem, all_send, taps_sem, gate_sem, back_sem, key_send, key_recv, value_send, value_recv,
):
    groups, length = twist.shape[1:]
    span = keys.shape[0]
    heads = queries.shape[1] // HEAD_DIM
    me = lax.axis_index("seq")
    core = me % CORES
    after, later = (me + 1) % GROUPS, (me + 2) % GROUPS
    barrier = pltpu.get_barrier_semaphore()

    def greet(turn, carry):
        pl.semaphore_signal(
            barrier, inc=1, device_id={"seq": peer_of(me, turn)}, device_id_type=MESH
        )
        return carry

    lax.fori_loop(0, GROUPS - 1, greet, 0)
    loads = [
        pltpu.make_async_copy(source, target, load_sem.at[i])
        for i, (source, target) in enumerate(
            [
                (filter_hbm, taps),
                (key_hbm, gate_key),
                (value_hbm, gate_value),
                (keys_hbm, keys.at[0]),
                (queries_hbm, queries),
                (query_hbm, gate),
            ]
        )
    ]
    for load in loads:
        load.start()
    loads[1].wait()
    loads[2].wait()
    gate_key[...] = gate_key[...] * gate_value[...]
    loads[0].wait()
    loads[3].wait()
    pl.semaphore_wait(barrier, GROUPS - 1)

    to_all(taps, got_taps, me, all_send.at[0], taps_sem)
    to_all(gate_key, got_gate, me, all_send.at[1], gate_sem)

    def block(ref):
        return lambda k: ref[pl.ds(k, groups, stride=CHANNELS), :]

    def store(k, value):
        convolved[pl.ds(k, groups, stride=CHANNELS), :] = value

    done(got_taps, taps_sem)
    spectrum[...] = to_spectrum(block(got_taps), ahead, twist, forward, high, low)
    done(got_gate, gate_sem)

    def pass_on(own, slots, send_sems, recv_sems):
        start_to(own, slots[2], later, send_sems[2], recv_sems[2])

        @pl.when(core == 0)
        def _():
            start_to(own, slots[1], after, send_sems[1], recv_sems[1])

    def relay(slots, send_sems, recv_sems):
        done(slots[2], recv_sems[2])

        @pl.when(core == 1)
        def _():
            start_to(slots[2], slots[1], me - 1, send_sems[1], recv_sems[1])

        start_to(slots[2], slots[3], after, send_sems[3], recv_sems[3])

    key_slots = [keys.at[o] for o in range(span)]
    key_sends = [key_send.at[o] for o in range(span)]
    key_recvs = [key_recv.at[o] for o in range(span)]
    pass_on(key_slots[0], key_slots, key_sends, key_recvs)
    signal = to_spectrum(block(got_gate), ahead, twist, forward, high, low)
    multiply_back(signal, spectrum[...], back, twist, inverse, high, low, store)
    to_all(convolved, got_back, me, all_send.at[2], back_sem.at[me // WIDE])
    relay(key_slots, key_sends, key_recvs)
    loads[4].wait()
    loads[5].wait()

    def part(head):
        rows = pl.ds(head * HEAD_DIM, HEAD_DIM)
        slots = [hyena.at[rows, :]] + [values.at[o, rows, :] for o in range(1, span)]
        sends = [value_send.at[o, head] for o in range(span)]
        recvs = [value_recv.at[o, head] for o in range(span)]
        return rows, slots, sends, recvs

    for head in range(heads):
        rows, slots, sends, recvs = part(head)
        done(got_back.at[rows, :], back_sem.at[head])
        hyena[rows, :] = gate[rows, :] * got_back[rows, :]
        pass_on(slots[0], slots, sends, recvs)

    allowed = [allowed_keys(key_blocks[...], me - o, o, length) for o in range(span)]
    done(key_slots[1], key_recvs[1])
    done(key_slots[3], key_recvs[3])
    for head in range(heads):
        cols = slice(head * HEAD_DIM, (head + 1) * HEAD_DIM)
        query = queries[:, cols] * HEAD_DIM ** (-0.5)
        scores = [
            jnp.where(allowed[o], dot_nt(query, keys[o, :, cols], EXACT), -1e30) for o in range(span)
        ]
        top = jnp.max(functools.reduce(jnp.maximum, scores), axis=1, keepdims=True)
        expo = [jnp.exp(s - top) for s in scores]
        total = jnp.sum(functools.reduce(jnp.add, expo), axis=1, keepdims=True)
        weight_high[head], weight_low[head] = split(jnp.concatenate(expo, axis=1) / total)
        rows, slots, sends, recvs = part(head)
        relay(slots, sends, recvs)

    for head in range(heads):
        rows, slots, sends, recvs = part(head)
        done(slots[1], recvs[1])
        done(slots[3], recvs[3])
        value_high, value_low = split(jnp.concatenate([slot[...] for slot in slots], axis=1))
        attended[:, head * HEAD_DIM : (head + 1) * HEAD_DIM] = (
            dot_nt(weight_high[head], value_high)
            + dot_nt(weight_low[head], value_high)
            + dot_nt(weight_high[head], value_low)
        )

    others = (GROUPS - 1) * CHANNELS
    for i, source in enumerate((taps, gate_key, convolved)):
        done(source.at[pl.ds(0, others), :], all_send.at[i])
    for o in range(1, span):
        done(key_slots[o], key_sends[o])
        for head in range(heads):
            rows, slots, sends, recvs = part(head)
            done(slots[o], sends[o])


def body(hyena_query, hyena_key, hyena_value, long_filter, queries, keys, key_blocks):
    channels, length = hyena_key.shape
    groups = lax.axis_size("seq")
    span = key_blocks.shape[1]
    heads = queries.shape[1] // HEAD_DIM
    tables = [jnp.asarray(t) for t in transform_tables(groups, length)]
    whole = pl.BlockSpec(memory_space=pl.ANY)
    local = pl.BlockSpec(memory_space=pltpu.VMEM)
    square = pltpu.VMEM((channels, length), jnp.float32)
    dma = pltpu.SemaphoreType.DMA
    rows = CHANNELS * groups
    return pl.pallas_call(
        kernel,
        out_shape=(
            jax.ShapeDtypeStruct(hyena_query.shape, jnp.float32),
            jax.ShapeDtypeStruct(queries.shape, jnp.float32),
        ),
        in_specs=[whole] * 6 + [local] * (1 + len(tables)),
        out_specs=(local, local),
        scratch_shapes=[
            square,
            square,
            square,
            square,
            pltpu.VMEM(queries.shape, jnp.float32),
            pltpu.VMEM((span, *keys.shape), jnp.float32),
            square,
            square,
            square,
            square,
            pltpu.VMEM((span, channels, length), jnp.float32),
            pltpu.VMEM((rows, 2 * length), jnp.bfloat16),
            pltpu.VMEM((rows, 2 * length), jnp.bfloat16),
            pltpu.VMEM((rows, 2 * length), jnp.float32),
            pltpu.VMEM((heads, length, span * length), jnp.bfloat16),
            pltpu.VMEM((heads, length, span * length), jnp.bfloat16),
            dma((6,)),
            dma((3,)),
            dma,
            dma,
            dma((heads,)),
            dma((span,)),
            dma((span,)),
            dma((span, heads)),
            dma((span, heads)),
        ],
        compiler_params=pltpu.CompilerParams(collective_id=0, has_side_effects=True),
    )(hyena_query, hyena_key, hyena_value, long_filter, queries, keys, key_blocks, *tables)


def solution(mesh):
    placed = (
        P("chan", "seq"),
        P("chan", "seq"),
        P("chan", "seq"),
        P("chan", "seq"),
        P("seq", "chan"),
        P("seq", "chan"),
        P("seq", None),
    )
    return jax.shard_map(
        body,
        mesh=mesh,
        in_specs=placed,
        out_specs=(P("chan", "seq"), P("seq", "chan")),
        check_vma=False,
    )
```

```python
import functools

import jax
import jax.numpy as jnp
import numpy as np
from jax import lax
from jax.experimental import pallas as pl
from jax.experimental.pallas import tpu as pltpu
from jax.sharding import PartitionSpec as P

HEAD_DIM = 128
EXACT = lax.Precision.HIGHEST
CHANNELS = 8


def split(value):
    high = value.astype(jnp.bfloat16)
    low = (value - high.astype(jnp.float32)).astype(jnp.bfloat16)
    return high, low


def dot(left, right):
    return jnp.dot(left, right, preferred_element_type=jnp.float32)


def dot_nt(left, right, precision=None):
    return lax.dot_general(
        left,
        right,
        (((1,), (1,)), ((), ())),
        precision=precision,
        preferred_element_type=jnp.float32,
    )


def split_table(table):
    high = table.astype(np.float32).astype(jnp.bfloat16)
    low = (table - high.astype(np.float64)).astype(np.float32).astype(jnp.bfloat16)
    return high, low


def transform_tables(groups, length):
    total = 2 * groups * length
    half = np.arange(groups)[:, None] + 0.5
    first = 2 * np.pi * half * np.arange(groups)[None, :] / (2 * groups)
    twist = 2 * np.pi * half * np.arange(length)[None, :] / total
    last = 2 * np.pi * np.arange(length)[:, None] * np.arange(length)[None, :] / length
    ahead = np.concatenate([np.cos(first), -np.sin(first)], axis=0)
    back = ahead.T * (2.0 / total)
    ahead_high, ahead_low = split_table(ahead)
    back_high, back_low = split_table(back)
    cosine, sine = np.cos(last), np.sin(last)
    forward = np.block([[cosine, -sine], [sine, cosine]])
    inverse = np.block([[cosine, sine], [-sine, cosine]])
    return (
        np.concatenate([ahead_high, ahead_high, ahead_low], axis=1),
        np.concatenate([back_high, back_high, back_low], axis=1),
        np.stack([np.cos(twist), np.sin(twist)]).astype(np.float32),
        np.stack(split_table(forward)),
        np.stack(split_table(inverse)),
    )


def three_pass(high_ref, low_ref, table_ref):
    high = high_ref[...]
    return dot(high, table_ref[0]) + dot(low_ref[...], table_ref[0]) + dot(high, table_ref[1])


def to_spectrum(block, ahead, twist, forward, high_ref, low_ref):
    groups, length = twist.shape[1:]
    twist_cos, twist_sin = twist[0], twist[1]
    for pair in range(CHANNELS // 2):
        high, low = split(jnp.concatenate([block(2 * pair), block(2 * pair + 1)], axis=1))
        mixed = dot(ahead[...], jnp.concatenate([high, low, high], axis=0))
        for side in range(2):
            real = mixed[:groups, side * length : (side + 1) * length]
            imag = mixed[groups:, side * length : (side + 1) * length]
            turned = jnp.concatenate(
                [real * twist_cos + imag * twist_sin, imag * twist_cos - real * twist_sin], axis=1
            )
            high, low = split(turned)
            rows = pl.ds((2 * pair + side) * groups, groups)
            high_ref[rows, :] = high
            low_ref[rows, :] = low
    return three_pass(high_ref, low_ref, forward)


def multiply_back(spectrum, other, back, twist, inverse, high_ref, low_ref, store):
    groups, length = twist.shape[1:]
    real = spectrum[:, :length] * other[:, :length] - spectrum[:, length:] * other[:, length:]
    imag = spectrum[:, :length] * other[:, length:] + spectrum[:, length:] * other[:, :length]
    high_ref[...], low_ref[...] = split(jnp.concatenate([real, imag], axis=1))
    mixed = three_pass(high_ref, low_ref, inverse)
    twist_cos, twist_sin = twist[0], twist[1]

    def turned(channel):
        part = mixed[channel * groups : (channel + 1) * groups]
        real, imag = part[:, :length], part[:, length:]
        return jnp.concatenate(
            [real * twist_cos - imag * twist_sin, imag * twist_cos + real * twist_sin], axis=0
        )

    for pair in range(CHANNELS // 2):
        high, low = split(jnp.concatenate([turned(2 * pair), turned(2 * pair + 1)], axis=1))
        signal = dot(back[...], jnp.concatenate([high, low, high], axis=0))
        store(2 * pair, signal[:, :length])
        store(2 * pair + 1, signal[:, length:])


def allowed_keys(key_blocks, source, offset, length):
    listed = jnp.max((key_blocks == source).astype(jnp.float32), axis=1, keepdims=True)
    listed = jnp.where(source >= 0, listed, 0.0) > 0.5
    if offset:
        return jnp.broadcast_to(listed, (length, length))
    rows = lax.broadcasted_iota(jnp.int32, (length, length), 0)
    cols = lax.broadcasted_iota(jnp.int32, (length, length), 1)
    return jnp.broadcast_to(listed, (length, length)) & (cols <= rows)


MESH = pl.DeviceIdType.MESH
X, Y, CORES = 4, 8, 2
GROUPS = X * Y * CORES


def terms(me):
    x = lax.div(me, Y * CORES)
    y = lax.rem(lax.div(me, CORES), Y)
    core = lax.rem(me, CORES)
    return x, [lax.rem(y + d, Y) * CORES for d in range(Y)], [core, 1 - core]


def for_others(parts, act):
    x, along, cores = parts
    reach = [d for far in range(Y // 2, 0, -1) for d in dict.fromkeys((far, Y - far))] + [0]

    def column(i, carry):
        base = lax.rem(x + 1 + i, X) * (Y * CORES)
        for d in reach:
            for c in range(CORES):
                act(base + along[d] + cores[c])
        return carry

    lax.fori_loop(0, X - 1, column, 0)
    for d in reach:
        for c in range(CORES):
            if d or c:
                act(x * (Y * CORES) + along[d] + cores[c])


def to_all(source, target, me, parts, send_sem, recv_sem):
    mine = pl.ds(pl.multiple_of(me * CHANNELS, CHANNELS), CHANNELS)

    def send(peer):
        rows = pl.ds(pl.multiple_of(peer * CHANNELS, CHANNELS), CHANNELS)
        start_to(source.at[rows, :], target.at[mine, :], peer, send_sem, recv_sem)

    for_others(parts, send)
    pltpu.make_async_copy(source.at[mine, :], target.at[mine, :], recv_sem).start()


def done(ref, sem):
    pltpu.make_async_copy(ref, ref, sem).wait()


def start_to(source, target, peer, send_sem, recv_sem):
    pltpu.make_async_remote_copy(
        src_ref=source,
        dst_ref=target,
        send_sem=send_sem,
        recv_sem=recv_sem,
        device_id={"seq": peer},
        device_id_type=MESH,
    ).start()


def kernel(
    query_hbm, key_hbm, value_hbm, filter_hbm, queries_hbm, keys_hbm, key_blocks_hbm,
    ahead_hbm, back_hbm, twist_hbm, forward_hbm, inverse_hbm,
    hyena, attended,
    gate, gate_key, gate_value, taps, queries, keys, key_blocks, ahead, back, twist, forward, inverse,
    got_taps, got_gate, convolved, got_back, values, high, low, spectrum, weight_high, weight_low,
    load_sem, all_send, taps_sem, gate_sem, back_sem, key_send, key_recv, value_send, value_recv,
):
    groups, length = twist.shape[1:]
    span = keys.shape[0]
    heads = queries.shape[1] // HEAD_DIM
    me = lax.axis_index("seq")
    parts = terms(me)
    core = parts[2][0]
    after, later = lax.rem(me + 1, GROUPS), lax.rem(me + 2, GROUPS)
    barrier = pltpu.get_barrier_semaphore()

    def greet(peer):
        pl.semaphore_signal(barrier, inc=1, device_id={"seq": peer}, device_id_type=MESH)

    for_others(parts, greet)
    sources = [
        filter_hbm, key_hbm, value_hbm, ahead_hbm, twist_hbm, forward_hbm,
        keys_hbm, back_hbm, inverse_hbm, query_hbm, queries_hbm, key_blocks_hbm,
    ]
    targets = [
        taps, gate_key, gate_value, ahead, twist, forward,
        keys.at[0], back, inverse, gate, queries, key_blocks,
    ]
    loads = [
        pltpu.make_async_copy(source, target, load_sem.at[i])
        for i, (source, target) in enumerate(zip(sources, targets))
    ]
    for load in loads:
        load.start()
    loads[1].wait()
    loads[2].wait()
    gate_key[...] = gate_key[...] * gate_value[...]
    loads[0].wait()
    pl.semaphore_wait(barrier, GROUPS - 1)

    to_all(taps, got_taps, me, parts, all_send.at[0], taps_sem)
    to_all(gate_key, got_gate, me, parts, all_send.at[1], gate_sem)
    for load in loads[3:]:
        load.wait()

    def block(ref):
        return lambda k: ref[pl.ds(k, groups, stride=CHANNELS), :]

    def store(k, value):
        convolved[pl.ds(k, groups, stride=CHANNELS), :] = value

    done(got_taps, taps_sem)
    spectrum[...] = to_spectrum(block(got_taps), ahead, twist, forward, high, low)
    done(got_gate, gate_sem)

    def pass_on(own, slots, send_sems, recv_sems):
        start_to(own, slots[2], later, send_sems[2], recv_sems[2])

        @pl.when(core == 0)
        def _():
            start_to(own, slots[1], after, send_sems[1], recv_sems[1])

    def relay(slots, send_sems, recv_sems):
        done(slots[2], recv_sems[2])

        @pl.when(core == 1)
        def _():
            start_to(slots[2], slots[1], me - 1, send_sems[1], recv_sems[1])

        start_to(slots[2], slots[3], after, send_sems[3], recv_sems[3])

    key_slots = [keys.at[o] for o in range(span)]
    key_sends = [key_send.at[o] for o in range(span)]
    key_recvs = [key_recv.at[o] for o in range(span)]
    pass_on(key_slots[0], key_slots, key_sends, key_recvs)
    signal = to_spectrum(block(got_gate), ahead, twist, forward, high, low)
    multiply_back(signal, spectrum[...], back, twist, inverse, high, low, store)
    to_all(convolved, got_back, me, parts, all_send.at[2], back_sem.at[parts[0]])
    relay(key_slots, key_sends, key_recvs)

    def part(head):
        rows = pl.ds(head * HEAD_DIM, HEAD_DIM)
        slots = [hyena.at[rows, :]] + [values.at[o, rows, :] for o in range(1, span)]
        sends = [value_send.at[o, head] for o in range(span)]
        recvs = [value_recv.at[o, head] for o in range(span)]
        return rows, slots, sends, recvs

    for head in range(heads):
        rows, slots, sends, recvs = part(head)
        done(got_back.at[rows, :], back_sem.at[head])
        hyena[rows, :] = gate[rows, :] * got_back[rows, :]
        pass_on(slots[0], slots, sends, recvs)

    allowed = [allowed_keys(key_blocks[...], me - o, o, length) for o in range(span)]
    done(key_slots[1], key_recvs[1])
    done(key_slots[3], key_recvs[3])
    for head in range(heads):
        cols = slice(head * HEAD_DIM, (head + 1) * HEAD_DIM)
        query = queries[:, cols] * HEAD_DIM ** (-0.5)
        scores = [
            jnp.where(allowed[o], dot_nt(query, keys[o, :, cols], EXACT), -1e30) for o in range(span)
        ]
        top = jnp.max(functools.reduce(jnp.maximum, scores), axis=1, keepdims=True)
        expo = [jnp.exp(s - top) for s in scores]
        total = jnp.sum(functools.reduce(jnp.add, expo), axis=1, keepdims=True)
        weight_high[head], weight_low[head] = split(jnp.concatenate(expo, axis=1) / total)
        rows, slots, sends, recvs = part(head)
        relay(slots, sends, recvs)

    for head in range(heads):
        rows, slots, sends, recvs = part(head)
        done(slots[1], recvs[1])
        done(slots[3], recvs[3])
        value_high, value_low = split(jnp.concatenate([slot[...] for slot in slots], axis=1))
        attended[:, head * HEAD_DIM : (head + 1) * HEAD_DIM] = (
            dot_nt(weight_high[head], value_high)
            + dot_nt(weight_low[head], value_high)
            + dot_nt(weight_high[head], value_low)
        )

    others = (GROUPS - 1) * CHANNELS
    for i, source in enumerate((taps, gate_key, convolved)):
        done(source.at[pl.ds(0, others), :], all_send.at[i])
    for o in range(1, span):
        done(key_slots[o], key_sends[o])
        for head in range(heads):
            rows, slots, sends, recvs = part(head)
            done(slots[o], sends[o])


def body(hyena_query, hyena_key, hyena_value, long_filter, queries, keys, key_blocks):
    channels, length = hyena_key.shape
    groups = lax.axis_size("seq")
    span = key_blocks.shape[1]
    heads = queries.shape[1] // HEAD_DIM
    tables = [jnp.asarray(t) for t in transform_tables(groups, length)]
    square = pltpu.VMEM((channels, length), jnp.float32)
    dma = pltpu.SemaphoreType.DMA
    rows = CHANNELS * groups
    operands = (hyena_query, hyena_key, hyena_value, long_filter, queries, keys, key_blocks, *tables)
    return pl.pallas_call(
        kernel,
        out_shape=(
            pltpu.VMEM(hyena_query.shape, jnp.float32),
            pltpu.VMEM(queries.shape, jnp.float32),
        ),
        in_specs=[pl.BlockSpec(memory_space=pltpu.HBM)] * len(operands),
        out_specs=(pl.BlockSpec(memory_space=pltpu.VMEM), pl.BlockSpec(memory_space=pltpu.VMEM)),
        scratch_shapes=[
            square,
            square,
            square,
            square,
            pltpu.VMEM(queries.shape, jnp.float32),
            pltpu.VMEM((span, *keys.shape), jnp.float32),
            pltpu.VMEM(key_blocks.shape, jnp.int32),
            *[pltpu.VMEM(t.shape, t.dtype) for t in tables],
            square,
            square,
            square,
            square,
            pltpu.VMEM((span, channels, length), jnp.float32),
            pltpu.VMEM((rows, 2 * length), jnp.bfloat16),
            pltpu.VMEM((rows, 2 * length), jnp.bfloat16),
            pltpu.VMEM((rows, 2 * length), jnp.float32),
            pltpu.VMEM((heads, length, span * length), jnp.bfloat16),
            pltpu.VMEM((heads, length, span * length), jnp.bfloat16),
            dma((len(operands),)),
            dma((3,)),
            dma,
            dma,
            dma((heads,)),
            dma((span,)),
            dma((span,)),
            dma((span, heads)),
            dma((span, heads)),
        ],
        compiler_params=pltpu.CompilerParams(collective_id=0, has_side_effects=True),
    )(*operands)


def solution(mesh):
    placed = (
        P("chan", "seq"),
        P("chan", "seq"),
        P("chan", "seq"),
        P("chan", "seq"),
        P("seq", "chan"),
        P("seq", "chan"),
        P("seq", None),
    )
    return jax.shard_map(
        body,
        mesh=mesh,
        in_specs=placed,
        out_specs=(P("chan", "seq"), P("seq", "chan")),
        check_vma=False,
    )
```

```python
import functools

import jax
import jax.numpy as jnp
import numpy as np
from jax import lax
from jax.experimental import pallas as pl
from jax.experimental.pallas import tpu as pltpu
from jax.sharding import PartitionSpec as P

HEAD_DIM = 128
EXACT = lax.Precision.HIGHEST
CHANNELS = 8


def split(value):
    high = value.astype(jnp.bfloat16)
    low = (value - high.astype(jnp.float32)).astype(jnp.bfloat16)
    return high, low


def dot(left, right):
    return jnp.dot(left, right, preferred_element_type=jnp.float32)


def dot_nt(left, right, precision=None):
    return lax.dot_general(
        left,
        right,
        (((1,), (1,)), ((), ())),
        precision=precision,
        preferred_element_type=jnp.float32,
    )


def split_table(table):
    high = table.astype(np.float32).astype(jnp.bfloat16)
    low = (table - high.astype(np.float64)).astype(np.float32).astype(jnp.bfloat16)
    return high, low


def transform_tables(groups, length):
    total = 2 * groups * length
    half = np.arange(groups)[:, None] + 0.5
    first = 2 * np.pi * half * np.arange(groups)[None, :] / (2 * groups)
    twist = 2 * np.pi * half * np.arange(length)[None, :] / total
    last = 2 * np.pi * np.arange(length)[:, None] * np.arange(length)[None, :] / length
    ahead = np.concatenate([np.cos(first), -np.sin(first)], axis=0)
    back = ahead.T * (2.0 / total)
    ahead_high, ahead_low = split_table(ahead)
    back_high, back_low = split_table(back)
    cosine, sine = np.cos(last), np.sin(last)
    forward = np.block([[cosine, -sine], [sine, cosine]])
    inverse = np.block([[cosine, sine], [-sine, cosine]])
    return (
        np.concatenate([ahead_high, ahead_high, ahead_low], axis=1),
        np.concatenate([back_high, back_high, back_low], axis=1),
        np.stack([np.cos(twist), np.sin(twist)]).astype(np.float32),
        np.stack(split_table(forward)),
        np.stack(split_table(inverse)),
    )


def three_pass(high_ref, low_ref, table_ref):
    high = high_ref[...]
    return dot(high, table_ref[0]) + dot(low_ref[...], table_ref[0]) + dot(high, table_ref[1])


def to_spectrum(block, ahead, twist, forward, high_ref, low_ref):
    groups, length = twist.shape[1:]
    twist_cos, twist_sin = twist[0], twist[1]
    for pair in range(CHANNELS // 2):
        high, low = split(jnp.concatenate([block(2 * pair), block(2 * pair + 1)], axis=1))
        mixed = dot(ahead[...], jnp.concatenate([high, low, high], axis=0))
        for side in range(2):
            real = mixed[:groups, side * length : (side + 1) * length]
            imag = mixed[groups:, side * length : (side + 1) * length]
            turned = jnp.concatenate(
                [real * twist_cos + imag * twist_sin, imag * twist_cos - real * twist_sin], axis=1
            )
            high, low = split(turned)
            rows = pl.ds((2 * pair + side) * groups, groups)
            high_ref[rows, :] = high
            low_ref[rows, :] = low
    return three_pass(high_ref, low_ref, forward)


def multiply_back(spectrum, other, back, twist, inverse, high_ref, low_ref, store):
    groups, length = twist.shape[1:]
    real = spectrum[:, :length] * other[:, :length] - spectrum[:, length:] * other[:, length:]
    imag = spectrum[:, :length] * other[:, length:] + spectrum[:, length:] * other[:, :length]
    high_ref[...], low_ref[...] = split(jnp.concatenate([real, imag], axis=1))
    mixed = three_pass(high_ref, low_ref, inverse)
    twist_cos, twist_sin = twist[0], twist[1]

    def turned(channel):
        part = mixed[channel * groups : (channel + 1) * groups]
        real, imag = part[:, :length], part[:, length:]
        return jnp.concatenate(
            [real * twist_cos - imag * twist_sin, imag * twist_cos + real * twist_sin], axis=0
        )

    for pair in range(CHANNELS // 2):
        high, low = split(jnp.concatenate([turned(2 * pair), turned(2 * pair + 1)], axis=1))
        signal = dot(back[...], jnp.concatenate([high, low, high], axis=0))
        store(2 * pair, signal[:, :length])
        store(2 * pair + 1, signal[:, length:])


def allowed_keys(key_blocks, source, offset, length):
    listed = jnp.max((key_blocks == source).astype(jnp.float32), axis=1, keepdims=True)
    listed = jnp.where(source >= 0, listed, 0.0) > 0.5
    if offset:
        return jnp.broadcast_to(listed, (length, length))
    rows = lax.broadcasted_iota(jnp.int32, (length, length), 0)
    cols = lax.broadcasted_iota(jnp.int32, (length, length), 1)
    return jnp.broadcast_to(listed, (length, length)) & (cols <= rows)


MESH = pl.DeviceIdType.MESH
X, Y, CORES = 4, 8, 2
GROUPS = X * Y * CORES


def terms(me):
    x = lax.div(me, Y * CORES)
    y = lax.rem(lax.div(me, CORES), Y)
    core = lax.rem(me, CORES)
    return x, [lax.rem(y + d, Y) * CORES for d in range(Y)], [core, 1 - core]


def for_others(parts, act):
    x, along, cores = parts
    reach = [d for far in range(Y // 2, 0, -1) for d in dict.fromkeys((far, Y - far))] + [0]

    def column(i, carry):
        base = lax.rem(x + 1 + i, X) * (Y * CORES)
        for d in reach:
            for c in range(CORES):
                act(base + along[d] + cores[c])
        return carry

    lax.fori_loop(0, X - 1, column, 0)
    for d in reach:
        for c in range(CORES):
            if d or c:
                act(x * (Y * CORES) + along[d] + cores[c])


def rows_of(device):
    return pl.ds(pl.multiple_of(device * CHANNELS, CHANNELS), CHANNELS)


def to_all(source, target, me, parts, send_sem, recv_sem, least=0):
    mine = rows_of(me)

    def send(peer):
        @pl.when(peer >= least)
        def _():
            start_to(source.at[rows_of(peer), :], target.at[mine, :], peer, send_sem, recv_sem)

    for_others(parts, send)
    pltpu.make_async_copy(source.at[mine, :], target.at[mine, :], recv_sem).start()


def done(ref, sem):
    pltpu.make_async_copy(ref, ref, sem).wait()


def start_to(source, target, peer, send_sem, recv_sem):
    pltpu.make_async_remote_copy(
        src_ref=source,
        dst_ref=target,
        send_sem=send_sem,
        recv_sem=recv_sem,
        device_id={"seq": peer},
        device_id_type=MESH,
    ).start()


def kernel(
    query_hbm, key_hbm, value_hbm, filter_hbm, queries_hbm, keys_hbm, key_blocks_hbm,
    ahead_hbm, back_hbm, twist_hbm, forward_hbm, inverse_hbm,
    hyena, attended,
    gate, gate_key, gate_value, taps, queries, keys, key_blocks, ahead, back, twist, forward, inverse,
    got_taps, got_gate, convolved, got_back, values, high, low, spectrum, weight_high, weight_low,
    here_sem, load_sem, all_send, taps_sem, gate_sem, back_sem, key_send, key_recv, value_send, value_recv,
):
    groups, length = twist.shape[1:]
    span = keys.shape[0]
    heads = queries.shape[1] // HEAD_DIM
    me = lax.axis_index("seq")
    parts = terms(me)
    core = parts[2][0]
    after, later = lax.rem(me + 1, GROUPS), lax.rem(me + 2, GROUPS)
    barrier = pltpu.get_barrier_semaphore()

    def greet(peer):
        pl.semaphore_signal(barrier, inc=1, device_id={"seq": peer}, device_id_type=MESH)

    @pl.when(me > 0)
    def _():
        for_others(parts, greet)

    sources = [
        filter_hbm, key_hbm, value_hbm, ahead_hbm, twist_hbm, forward_hbm,
        keys_hbm, back_hbm, inverse_hbm, query_hbm, queries_hbm, key_blocks_hbm,
    ]
    targets = [
        taps, gate_key, gate_value, ahead, twist, forward,
        keys.at[0], back, inverse, gate, queries, key_blocks,
    ]
    loads = [
        pltpu.make_async_copy(source, target, load_sem.at[i])
        for i, (source, target) in enumerate(zip(sources, targets))
    ]
    for load in loads:
        load.start()
    loads[1].wait()
    loads[2].wait()
    gate_key[...] = gate_key[...] * gate_value[...]
    loads[0].wait()

    @pl.when(me == 0)
    def _():
        pl.semaphore_wait(barrier, GROUPS - 1)
        for_others(
            parts,
            lambda peer: pl.semaphore_signal(
                here_sem, inc=1, device_id={"seq": peer}, device_id_type=MESH
            ),
        )

    @pl.when(me > 0)
    def _():
        pl.semaphore_wait(barrier, GROUPS - 2)

    to_all(taps, got_taps, me, parts, all_send.at[0], taps_sem, 1)
    to_all(gate_key, got_gate, me, parts, all_send.at[1], gate_sem, 1)

    @pl.when(me > 0)
    def _():
        pl.semaphore_wait(here_sem, 1)
        mine = rows_of(me)
        start_to(taps.at[rows_of(0), :], got_taps.at[mine, :], 0, all_send.at[0], taps_sem)
        start_to(gate_key.at[rows_of(0), :], got_gate.at[mine, :], 0, all_send.at[1], gate_sem)

    for load in loads[3:]:
        load.wait()

    def block(ref):
        return lambda k: ref[pl.ds(k, groups, stride=CHANNELS), :]

    def store(k, value):
        convolved[pl.ds(k, groups, stride=CHANNELS), :] = value

    def pass_on(own, slots, send_sems, recv_sems):
        start_to(own, slots[2], later, send_sems[2], recv_sems[2])

        @pl.when(core == 0)
        def _():
            start_to(own, slots[1], after, send_sems[1], recv_sems[1])

    def relay(slots, send_sems, recv_sems):
        done(slots[2], recv_sems[2])

        @pl.when(core == 1)
        def _():
            start_to(slots[2], slots[1], me - 1, send_sems[1], recv_sems[1])

        start_to(slots[2], slots[3], after, send_sems[3], recv_sems[3])

    key_slots = [keys.at[o] for o in range(span)]
    key_sends = [key_send.at[o] for o in range(span)]
    key_recvs = [key_recv.at[o] for o in range(span)]
    pass_on(key_slots[0], key_slots, key_sends, key_recvs)
    done(got_taps, taps_sem)
    spectrum[...] = to_spectrum(block(got_taps), ahead, twist, forward, high, low)
    done(got_gate, gate_sem)

    signal = to_spectrum(block(got_gate), ahead, twist, forward, high, low)
    multiply_back(signal, spectrum[...], back, twist, inverse, high, low, store)
    to_all(convolved, got_back, me, parts, all_send.at[2], back_sem.at[parts[0]])
    relay(key_slots, key_sends, key_recvs)

    def part(head):
        rows = pl.ds(head * HEAD_DIM, HEAD_DIM)
        slots = [hyena.at[rows, :]] + [values.at[o, rows, :] for o in range(1, span)]
        sends = [value_send.at[o, head] for o in range(span)]
        recvs = [value_recv.at[o, head] for o in range(span)]
        return rows, slots, sends, recvs

    for head in range(heads):
        rows, slots, sends, recvs = part(head)
        done(got_back.at[rows, :], back_sem.at[head])
        hyena[rows, :] = gate[rows, :] * got_back[rows, :]
        pass_on(slots[0], slots, sends, recvs)

    allowed = [allowed_keys(key_blocks[...], me - o, o, length) for o in range(span)]
    done(key_slots[1], key_recvs[1])
    done(key_slots[3], key_recvs[3])
    for head in range(heads):
        cols = slice(head * HEAD_DIM, (head + 1) * HEAD_DIM)
        query = queries[:, cols] * HEAD_DIM ** (-0.5)
        scores = [
            jnp.where(allowed[o], dot_nt(query, keys[o, :, cols], EXACT), -1e30) for o in range(span)
        ]
        top = jnp.max(functools.reduce(jnp.maximum, scores), axis=1, keepdims=True)
        expo = [jnp.exp(s - top) for s in scores]
        total = jnp.sum(functools.reduce(jnp.add, expo), axis=1, keepdims=True)
        weight_high[head], weight_low[head] = split(jnp.concatenate(expo, axis=1) / total)
        rows, slots, sends, recvs = part(head)
        relay(slots, sends, recvs)

    for head in range(heads):
        rows, slots, sends, recvs = part(head)
        done(slots[1], recvs[1])
        done(slots[3], recvs[3])
        value_high, value_low = split(jnp.concatenate([slot[...] for slot in slots], axis=1))
        attended[:, head * HEAD_DIM : (head + 1) * HEAD_DIM] = (
            dot_nt(weight_high[head], value_high)
            + dot_nt(weight_low[head], value_high)
            + dot_nt(weight_high[head], value_low)
        )

    others = (GROUPS - 1) * CHANNELS
    for i, source in enumerate((taps, gate_key, convolved)):
        done(source.at[pl.ds(0, others), :], all_send.at[i])
    for o in range(1, span):
        done(key_slots[o], key_sends[o])
        for head in range(heads):
            rows, slots, sends, recvs = part(head)
            done(slots[o], sends[o])


def body(hyena_query, hyena_key, hyena_value, long_filter, queries, keys, key_blocks):
    channels, length = hyena_key.shape
    groups = lax.axis_size("seq")
    span = key_blocks.shape[1]
    heads = queries.shape[1] // HEAD_DIM
    tables = [jnp.asarray(t) for t in transform_tables(groups, length)]
    square = pltpu.VMEM((channels, length), jnp.float32)
    dma = pltpu.SemaphoreType.DMA
    rows = CHANNELS * groups
    operands = (hyena_query, hyena_key, hyena_value, long_filter, queries, keys, key_blocks, *tables)
    return pl.pallas_call(
        kernel,
        out_shape=(
            pltpu.VMEM(hyena_query.shape, jnp.float32),
            pltpu.VMEM(queries.shape, jnp.float32),
        ),
        in_specs=[pl.BlockSpec(memory_space=pltpu.HBM)] * len(operands),
        out_specs=(pl.BlockSpec(memory_space=pltpu.VMEM), pl.BlockSpec(memory_space=pltpu.VMEM)),
        scratch_shapes=[
            square,
            square,
            square,
            square,
            pltpu.VMEM(queries.shape, jnp.float32),
            pltpu.VMEM((span, *keys.shape), jnp.float32),
            pltpu.VMEM(key_blocks.shape, jnp.int32),
            *[pltpu.VMEM(t.shape, t.dtype) for t in tables],
            square,
            square,
            square,
            square,
            pltpu.VMEM((span, channels, length), jnp.float32),
            pltpu.VMEM((rows, 2 * length), jnp.bfloat16),
            pltpu.VMEM((rows, 2 * length), jnp.bfloat16),
            pltpu.VMEM((rows, 2 * length), jnp.float32),
            pltpu.VMEM((heads, length, span * length), jnp.bfloat16),
            pltpu.VMEM((heads, length, span * length), jnp.bfloat16),
            pltpu.SemaphoreType.REGULAR,
            dma((len(operands),)),
            dma((3,)),
            dma,
            dma,
            dma((heads,)),
            dma((span,)),
            dma((span,)),
            dma((span, heads)),
            dma((span, heads)),
        ],
        compiler_params=pltpu.CompilerParams(collective_id=0, has_side_effects=True),
    )(*operands)


def solution(mesh):
    placed = (
        P("chan", "seq"),
        P("chan", "seq"),
        P("chan", "seq"),
        P("chan", "seq"),
        P("seq", "chan"),
        P("seq", "chan"),
        P("seq", None),
    )
    return jax.shard_map(
        body,
        mesh=mesh,
        in_specs=placed,
        out_specs=(P("chan", "seq"), P("seq", "chan")),
        check_vma=False,
    )
```

```python
import functools

import jax
import jax.numpy as jnp
import numpy as np
from jax import lax
from jax.experimental import pallas as pl
from jax.experimental.pallas import tpu as pltpu
from jax.sharding import PartitionSpec as P

HEAD_DIM = 128
EXACT = lax.Precision.HIGHEST
CHANNELS = 8


def split(value):
    high = value.astype(jnp.bfloat16)
    low = (value - high.astype(jnp.float32)).astype(jnp.bfloat16)
    return high, low


def dot(left, right):
    return jnp.dot(left, right, preferred_element_type=jnp.float32)


def dot_nt(left, right, precision=None):
    return lax.dot_general(
        left,
        right,
        (((1,), (1,)), ((), ())),
        precision=precision,
        preferred_element_type=jnp.float32,
    )


def split_table(table):
    high = table.astype(np.float32).astype(jnp.bfloat16)
    low = (table - high.astype(np.float64)).astype(np.float32).astype(jnp.bfloat16)
    return high, low


def transform_tables(groups, length):
    total = 2 * groups * length
    half = np.arange(groups)[:, None] + 0.5
    first = 2 * np.pi * half * np.arange(groups)[None, :] / (2 * groups)
    twist = 2 * np.pi * half * np.arange(length)[None, :] / total
    last = 2 * np.pi * np.arange(length)[:, None] * np.arange(length)[None, :] / length
    ahead = np.concatenate([np.cos(first), -np.sin(first)], axis=0)
    back = ahead.T * (2.0 / total)
    ahead_high, ahead_low = split_table(ahead)
    back_high, back_low = split_table(back)
    cosine, sine = np.cos(last), np.sin(last)
    forward = np.block([[cosine, -sine], [sine, cosine]])
    inverse = np.block([[cosine, sine], [-sine, cosine]])
    return (
        np.concatenate([ahead_high, ahead_high, ahead_low], axis=1),
        np.concatenate([back_high, back_high, back_low], axis=1),
        np.stack([np.cos(twist), np.sin(twist)]).astype(np.float32),
        np.stack(split_table(forward)),
        np.stack(split_table(inverse)),
    )


def three_pass(high_ref, low_ref, table_ref):
    high = high_ref[...]
    return dot(high, table_ref[0]) + dot(low_ref[...], table_ref[0]) + dot(high, table_ref[1])


def to_spectrum(block, ahead, twist, forward, high_ref, low_ref):
    groups, length = twist.shape[1:]
    twist_cos, twist_sin = twist[0], twist[1]
    for pair in range(CHANNELS // 2):
        high, low = split(jnp.concatenate([block(2 * pair), block(2 * pair + 1)], axis=1))
        mixed = dot(ahead[...], jnp.concatenate([high, low, high], axis=0))
        for side in range(2):
            real = mixed[:groups, side * length : (side + 1) * length]
            imag = mixed[groups:, side * length : (side + 1) * length]
            turned = jnp.concatenate(
                [real * twist_cos + imag * twist_sin, imag * twist_cos - real * twist_sin], axis=1
            )
            high, low = split(turned)
            rows = pl.ds((2 * pair + side) * groups, groups)
            high_ref[rows, :] = high
            low_ref[rows, :] = low
    return three_pass(high_ref, low_ref, forward)


def multiply_back(spectrum, other, back, twist, inverse, high_ref, low_ref, store):
    groups, length = twist.shape[1:]
    real = spectrum[:, :length] * other[:, :length] - spectrum[:, length:] * other[:, length:]
    imag = spectrum[:, :length] * other[:, length:] + spectrum[:, length:] * other[:, :length]
    high_ref[...], low_ref[...] = split(jnp.concatenate([real, imag], axis=1))
    mixed = three_pass(high_ref, low_ref, inverse)
    twist_cos, twist_sin = twist[0], twist[1]

    def turned(channel):
        part = mixed[channel * groups : (channel + 1) * groups]
        real, imag = part[:, :length], part[:, length:]
        return jnp.concatenate(
            [real * twist_cos - imag * twist_sin, imag * twist_cos + real * twist_sin], axis=0
        )

    for pair in range(CHANNELS // 2):
        high, low = split(jnp.concatenate([turned(2 * pair), turned(2 * pair + 1)], axis=1))
        signal = dot(back[...], jnp.concatenate([high, low, high], axis=0))
        store(2 * pair, signal[:, :length])
        store(2 * pair + 1, signal[:, length:])


def allowed_keys(key_blocks, source, offset, length):
    listed = jnp.max((key_blocks == source).astype(jnp.float32), axis=1, keepdims=True)
    listed = jnp.where(source >= 0, listed, 0.0) > 0.5
    if offset:
        return jnp.broadcast_to(listed, (length, length))
    rows = lax.broadcasted_iota(jnp.int32, (length, length), 0)
    cols = lax.broadcasted_iota(jnp.int32, (length, length), 1)
    return jnp.broadcast_to(listed, (length, length)) & (cols <= rows)


MESH = pl.DeviceIdType.MESH
X, Y, CORES = 4, 8, 2
GROUPS = X * Y * CORES


def terms(me):
    core = lax.rem(me, CORES)
    return lax.div(me, Y * CORES), lax.rem(lax.div(me, CORES), Y), [core, 1 - core]


def for_others(parts, act):
    x, y, cores = parts
    columns = [lax.rem(x + i, X) * (Y * CORES) for i in (2, 1, 3, 0)]

    def row(i, carry):
        half, odd = lax.div(i + 1, 2), lax.rem(i, 2)
        near = lax.rem(y + Y // 2 + half * (1 - 2 * odd), Y) * CORES
        for column in columns:
            for c in range(CORES):
                act(column + near + cores[c])
        return carry

    lax.fori_loop(0, Y - 1, row, 0)
    for column in columns[:-1]:
        for c in range(CORES):
            act(column + y * CORES + cores[c])
    act(columns[-1] + y * CORES + cores[1])


def rows_of(device):
    return pl.ds(pl.multiple_of(device * CHANNELS, CHANNELS), CHANNELS)


def to_all(source, target, me, parts, send_sem, recv_sem, least=0):
    mine = rows_of(me)

    def send(peer):
        @pl.when(peer >= least)
        def _():
            start_to(source.at[rows_of(peer), :], target.at[mine, :], peer, send_sem, recv_sem)

    for_others(parts, send)
    pltpu.make_async_copy(source.at[mine, :], target.at[mine, :], recv_sem).start()


def done(ref, sem):
    pltpu.make_async_copy(ref, ref, sem).wait()


def start_to(source, target, peer, send_sem, recv_sem):
    pltpu.make_async_remote_copy(
        src_ref=source,
        dst_ref=target,
        send_sem=send_sem,
        recv_sem=recv_sem,
        device_id={"seq": peer},
        device_id_type=MESH,
    ).start()


def kernel(
    query_hbm, key_hbm, value_hbm, filter_hbm, queries_hbm, keys_hbm, key_blocks_hbm,
    ahead_hbm, back_hbm, twist_hbm, forward_hbm, inverse_hbm,
    hyena, attended,
    gate, gate_key, gate_value, taps, queries, keys, key_blocks, ahead, back, twist, forward, inverse,
    got_taps, got_gate, convolved, got_back, values, high, low, spectrum, weight_high, weight_low,
    here_sem, load_sem, all_send, taps_sem, gate_sem, back_sem, key_send, key_recv, value_send, value_recv,
):
    groups, length = twist.shape[1:]
    span = keys.shape[0]
    heads = queries.shape[1] // HEAD_DIM
    me = lax.axis_index("seq")
    parts = terms(me)
    core = parts[2][0]
    after, later = lax.rem(me + 1, GROUPS), lax.rem(me + 2, GROUPS)
    barrier = pltpu.get_barrier_semaphore()

    def greet(peer):
        pl.semaphore_signal(barrier, inc=1, device_id={"seq": peer}, device_id_type=MESH)

    @pl.when(me > 0)
    def _():
        for_others(parts, greet)

    sources = [
        filter_hbm, key_hbm, value_hbm, ahead_hbm, twist_hbm, forward_hbm,
        keys_hbm, back_hbm, inverse_hbm, query_hbm, queries_hbm, key_blocks_hbm,
    ]
    targets = [
        taps, gate_key, gate_value, ahead, twist, forward,
        keys.at[0], back, inverse, gate, queries, key_blocks,
    ]
    loads = [
        pltpu.make_async_copy(source, target, load_sem.at[i])
        for i, (source, target) in enumerate(zip(sources, targets))
    ]
    for load in loads:
        load.start()
    @pl.when(me == 0)
    def _():
        pl.semaphore_wait(barrier, GROUPS - 1)
        for_others(
            parts,
            lambda peer: pl.semaphore_signal(
                here_sem, inc=1, device_id={"seq": peer}, device_id_type=MESH
            ),
        )

    loads[1].wait()
    loads[2].wait()
    gate_key[...] = gate_key[...] * gate_value[...]
    loads[0].wait()

    @pl.when(me > 0)
    def _():
        pl.semaphore_wait(barrier, GROUPS - 2)

    to_all(taps, got_taps, me, parts, all_send.at[0], taps_sem, 1)
    to_all(gate_key, got_gate, me, parts, all_send.at[1], gate_sem, 1)

    @pl.when(me > 0)
    def _():
        pl.semaphore_wait(here_sem, 1)
        mine = rows_of(me)
        start_to(taps.at[rows_of(0), :], got_taps.at[mine, :], 0, all_send.at[0], taps_sem)
        start_to(gate_key.at[rows_of(0), :], got_gate.at[mine, :], 0, all_send.at[1], gate_sem)

    for load in loads[3:]:
        load.wait()

    def block(ref):
        return lambda k: ref[pl.ds(k, groups, stride=CHANNELS), :]

    def store(k, value):
        convolved[pl.ds(k, groups, stride=CHANNELS), :] = value

    def pass_on(own, slots, send_sems, recv_sems):
        start_to(own, slots[2], later, send_sems[2], recv_sems[2])

        @pl.when(core == 0)
        def _():
            start_to(own, slots[1], after, send_sems[1], recv_sems[1])

    def relay(slots, send_sems, recv_sems):
        done(slots[2], recv_sems[2])

        @pl.when(core == 1)
        def _():
            start_to(slots[2], slots[1], me - 1, send_sems[1], recv_sems[1])

        start_to(slots[2], slots[3], after, send_sems[3], recv_sems[3])

    key_slots = [keys.at[o] for o in range(span)]
    key_sends = [key_send.at[o] for o in range(span)]
    key_recvs = [key_recv.at[o] for o in range(span)]
    pass_on(key_slots[0], key_slots, key_sends, key_recvs)
    done(got_taps, taps_sem)
    spectrum[...] = to_spectrum(block(got_taps), ahead, twist, forward, high, low)
    done(got_gate, gate_sem)

    signal = to_spectrum(block(got_gate), ahead, twist, forward, high, low)
    multiply_back(signal, spectrum[...], back, twist, inverse, high, low, store)
    to_all(convolved, got_back, me, parts, all_send.at[2], back_sem.at[parts[0]])
    relay(key_slots, key_sends, key_recvs)

    def part(head):
        rows = pl.ds(head * HEAD_DIM, HEAD_DIM)
        slots = [hyena.at[rows, :]] + [values.at[o, rows, :] for o in range(1, span)]
        sends = [value_send.at[o, head] for o in range(span)]
        recvs = [value_recv.at[o, head] for o in range(span)]
        return rows, slots, sends, recvs

    for head in range(heads):
        rows, slots, sends, recvs = part(head)
        done(got_back.at[rows, :], back_sem.at[head])
        hyena[rows, :] = gate[rows, :] * got_back[rows, :]
        pass_on(slots[0], slots, sends, recvs)

    allowed = [allowed_keys(key_blocks[...], me - o, o, length) for o in range(span)]
    done(key_slots[1], key_recvs[1])
    done(key_slots[3], key_recvs[3])
    for head in range(heads):
        cols = slice(head * HEAD_DIM, (head + 1) * HEAD_DIM)
        query = queries[:, cols] * HEAD_DIM ** (-0.5)
        scores = [
            jnp.where(allowed[o], dot_nt(query, keys[o, :, cols], EXACT), -1e30) for o in range(span)
        ]
        top = jnp.max(functools.reduce(jnp.maximum, scores), axis=1, keepdims=True)
        expo = [jnp.exp(s - top) for s in scores]
        total = jnp.sum(functools.reduce(jnp.add, expo), axis=1, keepdims=True)
        weight_high[head], weight_low[head] = split(jnp.concatenate(expo, axis=1) / total)
        rows, slots, sends, recvs = part(head)
        relay(slots, sends, recvs)

    for head in range(heads):
        rows, slots, sends, recvs = part(head)
        done(slots[1], recvs[1])
        done(slots[3], recvs[3])
        value_high, value_low = split(jnp.concatenate([slot[...] for slot in slots], axis=1))
        attended[:, head * HEAD_DIM : (head + 1) * HEAD_DIM] = (
            dot_nt(weight_high[head], value_high)
            + dot_nt(weight_low[head], value_high)
            + dot_nt(weight_high[head], value_low)
        )

    others = (GROUPS - 1) * CHANNELS
    for i, source in enumerate((taps, gate_key, convolved)):
        done(source.at[pl.ds(0, others), :], all_send.at[i])
    for o in range(1, span):
        done(key_slots[o], key_sends[o])
        for head in range(heads):
            rows, slots, sends, recvs = part(head)
            done(slots[o], sends[o])


def body(hyena_query, hyena_key, hyena_value, long_filter, queries, keys, key_blocks):
    channels, length = hyena_key.shape
    groups = lax.axis_size("seq")
    span = key_blocks.shape[1]
    heads = queries.shape[1] // HEAD_DIM
    tables = [jnp.asarray(t) for t in transform_tables(groups, length)]
    square = pltpu.VMEM((channels, length), jnp.float32)
    dma = pltpu.SemaphoreType.DMA
    rows = CHANNELS * groups
    operands = (hyena_query, hyena_key, hyena_value, long_filter, queries, keys, key_blocks, *tables)
    return pl.pallas_call(
        kernel,
        out_shape=(
            pltpu.VMEM(hyena_query.shape, jnp.float32),
            pltpu.VMEM(queries.shape, jnp.float32),
        ),
        in_specs=[pl.BlockSpec(memory_space=pltpu.HBM)] * len(operands),
        out_specs=(pl.BlockSpec(memory_space=pltpu.VMEM), pl.BlockSpec(memory_space=pltpu.VMEM)),
        scratch_shapes=[
            square,
            square,
            square,
            square,
            pltpu.VMEM(queries.shape, jnp.float32),
            pltpu.VMEM((span, *keys.shape), jnp.float32),
            pltpu.VMEM(key_blocks.shape, jnp.int32),
            *[pltpu.VMEM(t.shape, t.dtype) for t in tables],
            square,
            square,
            square,
            square,
            pltpu.VMEM((span, channels, length), jnp.float32),
            pltpu.VMEM((rows, 2 * length), jnp.bfloat16),
            pltpu.VMEM((rows, 2 * length), jnp.bfloat16),
            pltpu.VMEM((rows, 2 * length), jnp.float32),
            pltpu.VMEM((heads, length, span * length), jnp.bfloat16),
            pltpu.VMEM((heads, length, span * length), jnp.bfloat16),
            pltpu.SemaphoreType.REGULAR,
            dma((len(operands),)),
            dma((3,)),
            dma,
            dma,
            dma((heads,)),
            dma((span,)),
            dma((span,)),
            dma((span, heads)),
            dma((span, heads)),
        ],
        compiler_params=pltpu.CompilerParams(collective_id=0, has_side_effects=True),
    )(*operands)


def solution(mesh):
    placed = (
        P("chan", "seq"),
        P("chan", "seq"),
        P("chan", "seq"),
        P("chan", "seq"),
        P("seq", "chan"),
        P("seq", "chan"),
        P("seq", None),
    )
    return jax.shard_map(
        body,
        mesh=mesh,
        in_specs=placed,
        out_specs=(P("chan", "seq"), P("seq", "chan")),
        check_vma=False,
    )
```

```python
import functools

import jax
import jax.numpy as jnp
import numpy as np
from jax import lax
from jax.experimental import pallas as pl
from jax.experimental.pallas import tpu as pltpu
from jax.sharding import PartitionSpec as P

HEAD_DIM = 128
EXACT = lax.Precision.HIGHEST
CHANNELS = 8


def split(value):
    high = value.astype(jnp.bfloat16)
    low = (value - high.astype(jnp.float32)).astype(jnp.bfloat16)
    return high, low


def dot(left, right):
    return jnp.dot(left, right, preferred_element_type=jnp.float32)


def dot_nt(left, right, precision=None):
    return lax.dot_general(
        left,
        right,
        (((1,), (1,)), ((), ())),
        precision=precision,
        preferred_element_type=jnp.float32,
    )


def split_table(table):
    high = table.astype(np.float32).astype(jnp.bfloat16)
    low = (table - high.astype(np.float64)).astype(np.float32).astype(jnp.bfloat16)
    return high, low


def transform_tables(groups, length):
    total = 2 * groups * length
    half = np.arange(groups)[:, None] + 0.5
    first = 2 * np.pi * half * np.arange(groups)[None, :] / (2 * groups)
    twist = 2 * np.pi * half * np.arange(length)[None, :] / total
    last = 2 * np.pi * np.arange(length)[:, None] * np.arange(length)[None, :] / length
    ahead = np.concatenate([np.cos(first), -np.sin(first)], axis=0)
    back = ahead.T * (2.0 / total)
    ahead_high, ahead_low = split_table(ahead)
    back_high, back_low = split_table(back)
    cosine, sine = np.cos(last), np.sin(last)
    forward = np.block([[cosine, -sine], [sine, cosine]])
    inverse = np.block([[cosine, sine], [-sine, cosine]])
    return (
        np.concatenate([ahead_high, ahead_high, ahead_low], axis=1),
        np.concatenate([back_high, back_high, back_low], axis=1),
        np.stack([np.cos(twist), np.sin(twist)]).astype(np.float32),
        np.stack(split_table(forward)),
        np.stack(split_table(inverse)),
    )


def three_pass(high_ref, low_ref, table_ref):
    high = high_ref[...]
    return dot(high, table_ref[0]) + dot(low_ref[...], table_ref[0]) + dot(high, table_ref[1])


def to_spectrum(block, ahead, twist, forward, high_ref, low_ref):
    groups, length = twist.shape[1:]
    twist_cos, twist_sin = twist[0], twist[1]
    for pair in range(CHANNELS // 2):
        high, low = split(jnp.concatenate([block(2 * pair), block(2 * pair + 1)], axis=1))
        mixed = dot(ahead[...], jnp.concatenate([high, low, high], axis=0))
        for side in range(2):
            real = mixed[:groups, side * length : (side + 1) * length]
            imag = mixed[groups:, side * length : (side + 1) * length]
            turned = jnp.concatenate(
                [real * twist_cos + imag * twist_sin, imag * twist_cos - real * twist_sin], axis=1
            )
            high, low = split(turned)
            rows = pl.ds((2 * pair + side) * groups, groups)
            high_ref[rows, :] = high
            low_ref[rows, :] = low
    return three_pass(high_ref, low_ref, forward)


def multiply_back(spectrum, other, back, twist, inverse, high_ref, low_ref, store):
    groups, length = twist.shape[1:]
    real = spectrum[:, :length] * other[:, :length] - spectrum[:, length:] * other[:, length:]
    imag = spectrum[:, :length] * other[:, length:] + spectrum[:, length:] * other[:, :length]
    high_ref[...], low_ref[...] = split(jnp.concatenate([real, imag], axis=1))
    mixed = three_pass(high_ref, low_ref, inverse)
    twist_cos, twist_sin = twist[0], twist[1]

    def turned(channel):
        part = mixed[channel * groups : (channel + 1) * groups]
        real, imag = part[:, :length], part[:, length:]
        return jnp.concatenate(
            [real * twist_cos - imag * twist_sin, imag * twist_cos + real * twist_sin], axis=0
        )

    for pair in range(CHANNELS // 2):
        high, low = split(jnp.concatenate([turned(2 * pair), turned(2 * pair + 1)], axis=1))
        signal = dot(back[...], jnp.concatenate([high, low, high], axis=0))
        store(2 * pair, signal[:, :length])
        store(2 * pair + 1, signal[:, length:])


def allowed_keys(key_blocks, source, offset, length):
    listed = jnp.max((key_blocks == source).astype(jnp.float32), axis=1, keepdims=True)
    listed = jnp.where(source >= 0, listed, 0.0) > 0.5
    if offset:
        return jnp.broadcast_to(listed, (length, length))
    rows = lax.broadcasted_iota(jnp.int32, (length, length), 0)
    cols = lax.broadcasted_iota(jnp.int32, (length, length), 1)
    return jnp.broadcast_to(listed, (length, length)) & (cols <= rows)


MESH = pl.DeviceIdType.MESH
X, Y, CORES = 4, 8, 2
GROUPS = X * Y * CORES


def terms(me):
    core = lax.rem(me, CORES)
    return lax.div(me, Y * CORES), lax.rem(lax.div(me, CORES), Y), [core, 1 - core]


def for_others(parts, act):
    x, y, cores = parts
    columns = [lax.rem(x + i, X) * (Y * CORES) for i in (2, 1, 3, 0)]

    def row(i, carry):
        half, odd = lax.div(i + 1, 2), lax.rem(i, 2)
        near = lax.rem(y + Y // 2 + half * (1 - 2 * odd), Y) * CORES
        for column in columns:
            for c in range(CORES):
                act(column + near + cores[c])
        return carry

    lax.fori_loop(0, Y - 1, row, 0)
    for column in columns[:-1]:
        for c in range(CORES):
            act(column + y * CORES + cores[c])
    act(columns[-1] + y * CORES + cores[1])


COLUMNS = (1, 2, 3, 0)


def by_column(parts, act):
    x, y, cores = parts

    def rows(column, least):
        for far in range(Y // 2, 0, -1):
            for d in dict.fromkeys((far, Y - far)):
                for c in range(CORES):
                    act(column + lax.rem(y + d, Y) * CORES + cores[c])
        for c in range(least, CORES):
            act(column + y * CORES + cores[c])

    def other(i, carry):
        rows(lax.rem(x + 1 + i, X) * (Y * CORES), 0)
        return carry

    lax.fori_loop(0, X - 1, other, 0)
    rows(x * (Y * CORES), 1)


def rows_of(device):
    return pl.ds(pl.multiple_of(device * CHANNELS, CHANNELS), CHANNELS)


def to_all(source, target, me, parts, send_sem, recv_sem, least=0, others=for_others):
    mine = rows_of(me)

    def send(peer):
        @pl.when(peer >= least)
        def _():
            start_to(source.at[rows_of(peer), :], target.at[mine, :], peer, send_sem, recv_sem)

    others(parts, send)
    pltpu.make_async_copy(source.at[mine, :], target.at[mine, :], recv_sem).start()


def done(ref, sem):
    pltpu.make_async_copy(ref, ref, sem).wait()


def start_to(source, target, peer, send_sem, recv_sem):
    pltpu.make_async_remote_copy(
        src_ref=source,
        dst_ref=target,
        send_sem=send_sem,
        recv_sem=recv_sem,
        device_id={"seq": peer},
        device_id_type=MESH,
    ).start()


def kernel(
    query_hbm, key_hbm, value_hbm, filter_hbm, queries_hbm, keys_hbm, key_blocks_hbm,
    ahead_hbm, back_hbm, twist_hbm, forward_hbm, inverse_hbm,
    hyena, attended,
    gate, gate_key, gate_value, taps, queries, keys, key_blocks, ahead, back, twist, forward, inverse,
    got_taps, got_gate, convolved, got_back, values, high, low, spectrum, weight_high, weight_low,
    here_sem, load_sem, all_send, taps_sem, gate_sem, back_sem, key_send, key_recv, value_send, value_recv,
):
    groups, length = twist.shape[1:]
    span = keys.shape[0]
    heads = queries.shape[1] // HEAD_DIM
    me = lax.axis_index("seq")
    parts = terms(me)
    core = parts[2][0]
    after, later = lax.rem(me + 1, GROUPS), lax.rem(me + 2, GROUPS)
    barrier = pltpu.get_barrier_semaphore()

    def greet(peer):
        pl.semaphore_signal(barrier, inc=1, device_id={"seq": peer}, device_id_type=MESH)

    @pl.when(me > 0)
    def _():
        for_others(parts, greet)

    sources = [
        filter_hbm, key_hbm, value_hbm, ahead_hbm, twist_hbm, forward_hbm,
        keys_hbm, back_hbm, inverse_hbm, query_hbm, queries_hbm, key_blocks_hbm,
    ]
    targets = [
        taps, gate_key, gate_value, ahead, twist, forward,
        keys.at[0], back, inverse, gate, queries, key_blocks,
    ]
    loads = [
        pltpu.make_async_copy(source, target, load_sem.at[i])
        for i, (source, target) in enumerate(zip(sources, targets))
    ]
    for load in loads:
        load.start()
    @pl.when(me == 0)
    def _():
        pl.semaphore_wait(barrier, GROUPS - 1)
        for_others(
            parts,
            lambda peer: pl.semaphore_signal(
                here_sem, inc=1, device_id={"seq": peer}, device_id_type=MESH
            ),
        )

    loads[1].wait()
    loads[2].wait()
    gate_key[...] = gate_key[...] * gate_value[...]
    loads[0].wait()

    @pl.when(me > 0)
    def _():
        pl.semaphore_wait(barrier, GROUPS - 2)

    to_all(taps, got_taps, me, parts, all_send.at[0], taps_sem, 1)
    to_all(gate_key, got_gate, me, parts, all_send.at[1], gate_sem, 1)

    @pl.when(me > 0)
    def _():
        pl.semaphore_wait(here_sem, 1)
        mine = rows_of(me)
        start_to(taps.at[rows_of(0), :], got_taps.at[mine, :], 0, all_send.at[0], taps_sem)
        start_to(gate_key.at[rows_of(0), :], got_gate.at[mine, :], 0, all_send.at[1], gate_sem)

    for load in loads[3:]:
        load.wait()

    def block(ref):
        return lambda k: ref[pl.ds(k, groups, stride=CHANNELS), :]

    def store(k, value):
        convolved[pl.ds(k, groups, stride=CHANNELS), :] = value

    def pass_on(own, slots, send_sems, recv_sems):
        start_to(own, slots[2], later, send_sems[2], recv_sems[2])

        @pl.when(core == 0)
        def _():
            start_to(own, slots[1], after, send_sems[1], recv_sems[1])

    def relay(slots, send_sems, recv_sems):
        done(slots[2], recv_sems[2])

        @pl.when(core == 1)
        def _():
            start_to(slots[2], slots[1], me - 1, send_sems[1], recv_sems[1])

        start_to(slots[2], slots[3], after, send_sems[3], recv_sems[3])

    key_slots = [keys.at[o] for o in range(span)]
    key_sends = [key_send.at[o] for o in range(span)]
    key_recvs = [key_recv.at[o] for o in range(span)]
    pass_on(key_slots[0], key_slots, key_sends, key_recvs)
    done(got_taps, taps_sem)
    spectrum[...] = to_spectrum(block(got_taps), ahead, twist, forward, high, low)
    done(got_gate, gate_sem)

    signal = to_spectrum(block(got_gate), ahead, twist, forward, high, low)
    multiply_back(signal, spectrum[...], back, twist, inverse, high, low, store)
    to_all(convolved, got_back, me, parts, all_send.at[2], back_sem.at[parts[0]], 0, by_column)
    relay(key_slots, key_sends, key_recvs)

    def in_turn(device):
        x = lax.div(device, Y * CORES)
        return [lax.rem(x + X - turn, X) for turn in COLUMNS]

    def part(head):
        rows = pl.ds(pl.multiple_of(head * HEAD_DIM, HEAD_DIM), HEAD_DIM)
        slots = [hyena.at[rows, :]] + [values.at[o, rows, :] for o in range(1, span)]
        sends = [value_send.at[o, head] for o in range(span)]
        recvs = [value_recv.at[o, head] for o in range(span)]
        return rows, slots, sends, recvs

    for head in in_turn(me):
        rows, slots, sends, recvs = part(head)
        done(got_back.at[rows, :], back_sem.at[head])
        hyena[rows, :] = gate[rows, :] * got_back[rows, :]
        pass_on(slots[0], slots, sends, recvs)

    allowed = [allowed_keys(key_blocks[...], me - o, o, length) for o in range(span)]
    done(key_slots[1], key_recvs[1])
    done(key_slots[3], key_recvs[3])
    for head in in_turn(lax.rem(me + GROUPS - 2, GROUPS)):
        rows, slots, sends, recvs = part(head)
        query = queries[:, rows] * HEAD_DIM ** (-0.5)
        scores = [
            jnp.where(allowed[o], dot_nt(query, keys[o, :, rows], EXACT), -1e30) for o in range(span)
        ]
        top = jnp.max(functools.reduce(jnp.maximum, scores), axis=1, keepdims=True)
        expo = [jnp.exp(s - top) for s in scores]
        total = jnp.sum(functools.reduce(jnp.add, expo), axis=1, keepdims=True)
        weight_high[head], weight_low[head] = split(jnp.concatenate(expo, axis=1) / total)
        relay(slots, sends, recvs)

    for head in in_turn(lax.rem(me + GROUPS - 3, GROUPS)):
        rows, slots, sends, recvs = part(head)
        done(slots[1], recvs[1])
        done(slots[3], recvs[3])
        value_high, value_low = split(jnp.concatenate([slot[...] for slot in slots], axis=1))
        attended[:, rows] = (
            dot_nt(weight_high[head], value_high)
            + dot_nt(weight_low[head], value_high)
            + dot_nt(weight_high[head], value_low)
        )

    others = (GROUPS - 1) * CHANNELS
    for i, source in enumerate((taps, gate_key, convolved)):
        done(source.at[pl.ds(0, others), :], all_send.at[i])
    for o in range(1, span):
        done(key_slots[o], key_sends[o])
        for head in range(heads):
            rows, slots, sends, recvs = part(head)
            done(slots[o], sends[o])


def write_kernel(hyena, attended, hyena_hbm, attended_hbm, sem):
    copies = [
        pltpu.make_async_copy(hyena, hyena_hbm, sem.at[0]),
        pltpu.make_async_copy(attended, attended_hbm, sem.at[1]),
    ]
    for copy in copies:
        copy.start()
    for copy in copies:
        copy.wait()


def body(hyena_query, hyena_key, hyena_value, long_filter, queries, keys, key_blocks):
    channels, length = hyena_key.shape
    groups = lax.axis_size("seq")
    span = key_blocks.shape[1]
    heads = queries.shape[1] // HEAD_DIM
    tables = [jnp.asarray(t) for t in transform_tables(groups, length)]
    square = pltpu.VMEM((channels, length), jnp.float32)
    dma = pltpu.SemaphoreType.DMA
    rows = CHANNELS * groups
    operands = (hyena_query, hyena_key, hyena_value, long_filter, queries, keys, key_blocks, *tables)
    results = pl.pallas_call(
        kernel,
        out_shape=(
            pltpu.VMEM(hyena_query.shape, jnp.float32),
            pltpu.VMEM(queries.shape, jnp.float32),
        ),
        in_specs=[pl.BlockSpec(memory_space=pltpu.HBM)] * len(operands),
        out_specs=(pl.BlockSpec(memory_space=pltpu.VMEM), pl.BlockSpec(memory_space=pltpu.VMEM)),
        scratch_shapes=[
            square,
            square,
            square,
            square,
            pltpu.VMEM(queries.shape, jnp.float32),
            pltpu.VMEM((span, *keys.shape), jnp.float32),
            pltpu.VMEM(key_blocks.shape, jnp.int32),
            *[pltpu.VMEM(t.shape, t.dtype) for t in tables],
            square,
            square,
            square,
            square,
            pltpu.VMEM((span, channels, length), jnp.float32),
            pltpu.VMEM((rows, 2 * length), jnp.bfloat16),
            pltpu.VMEM((rows, 2 * length), jnp.bfloat16),
            pltpu.VMEM((rows, 2 * length), jnp.float32),
            pltpu.VMEM((heads, length, span * length), jnp.bfloat16),
            pltpu.VMEM((heads, length, span * length), jnp.bfloat16),
            pltpu.SemaphoreType.REGULAR,
            dma((len(operands),)),
            dma((3,)),
            dma,
            dma,
            dma((heads,)),
            dma((span,)),
            dma((span,)),
            dma((span, heads)),
            dma((span, heads)),
        ],
        compiler_params=pltpu.CompilerParams(collective_id=0, has_side_effects=True),
    )(*operands)
    return pl.pallas_call(
        write_kernel,
        out_shape=tuple(jax.ShapeDtypeStruct(r.shape, r.dtype) for r in results),
        in_specs=[pl.BlockSpec(memory_space=pl.ANY)] * 2,
        out_specs=[pl.BlockSpec(memory_space=pltpu.HBM)] * 2,
        scratch_shapes=[dma((2,))],
        compiler_params=pltpu.CompilerParams(vmem_limit_bytes=1 << 20),
    )(*results)


def solution(mesh):
    placed = (
        P("chan", "seq"),
        P("chan", "seq"),
        P("chan", "seq"),
        P("chan", "seq"),
        P("seq", "chan"),
        P("seq", "chan"),
        P("seq", None),
    )
    return jax.shard_map(
        body,
        mesh=mesh,
        in_specs=placed,
        out_specs=(P("chan", "seq"), P("seq", "chan")),
        check_vma=False,
    )
```

```python
import functools

import jax
import jax.numpy as jnp
import numpy as np
from jax import lax
from jax.experimental import pallas as pl
from jax.experimental.pallas import tpu as pltpu
from jax.sharding import PartitionSpec as P

HEAD_DIM = 128
EXACT = lax.Precision.HIGHEST
CHANNELS = 8


def split(value):
    high = value.astype(jnp.bfloat16)
    low = (value - high.astype(jnp.float32)).astype(jnp.bfloat16)
    return high, low


def dot(left, right):
    return jnp.dot(left, right, preferred_element_type=jnp.float32)


def dot_nt(left, right, precision=None):
    return lax.dot_general(
        left,
        right,
        (((1,), (1,)), ((), ())),
        precision=precision,
        preferred_element_type=jnp.float32,
    )


def split_table(table):
    high = table.astype(np.float32).astype(jnp.bfloat16)
    low = (table - high.astype(np.float64)).astype(np.float32).astype(jnp.bfloat16)
    return high, low


def transform_tables(groups, length):
    total = 2 * groups * length
    half = np.arange(groups)[:, None] + 0.5
    first = 2 * np.pi * half * np.arange(groups)[None, :] / (2 * groups)
    twist = 2 * np.pi * half * np.arange(length)[None, :] / total
    last = 2 * np.pi * np.arange(length)[:, None] * np.arange(length)[None, :] / length
    ahead = np.concatenate([np.cos(first), -np.sin(first)], axis=0)
    back = ahead.T * (2.0 / total)
    ahead_high, ahead_low = split_table(ahead)
    back_high, back_low = split_table(back)
    cosine, sine = np.cos(last), np.sin(last)
    forward = np.block([[cosine, -sine], [sine, cosine]])
    inverse = np.block([[cosine, sine], [-sine, cosine]])
    return (
        np.concatenate([ahead_high, ahead_high, ahead_low], axis=1),
        np.concatenate([back_high, back_high, back_low], axis=1),
        np.stack([np.cos(twist), np.sin(twist)]).astype(np.float32),
        np.stack(split_table(forward)),
        np.stack(split_table(inverse)),
    )


def three_pass(high_ref, low_ref, table_ref):
    high = high_ref[...]
    return dot(high, table_ref[0]) + dot(low_ref[...], table_ref[0]) + dot(high, table_ref[1])


def to_spectrum(block, ahead, twist, forward, high_ref, low_ref):
    groups, length = twist.shape[1:]
    twist_cos, twist_sin = twist[0], twist[1]
    for pair in range(CHANNELS // 2):
        high, low = split(jnp.concatenate([block(2 * pair), block(2 * pair + 1)], axis=1))
        mixed = dot(ahead[...], jnp.concatenate([high, low, high], axis=0))
        for side in range(2):
            real = mixed[:groups, side * length : (side + 1) * length]
            imag = mixed[groups:, side * length : (side + 1) * length]
            turned = jnp.concatenate(
                [real * twist_cos + imag * twist_sin, imag * twist_cos - real * twist_sin], axis=1
            )
            high, low = split(turned)
            rows = pl.ds((2 * pair + side) * groups, groups)
            high_ref[rows, :] = high
            low_ref[rows, :] = low
    return three_pass(high_ref, low_ref, forward)


def multiply_back(spectrum, other, back, twist, inverse, high_ref, low_ref, store):
    groups, length = twist.shape[1:]
    real = spectrum[:, :length] * other[:, :length] - spectrum[:, length:] * other[:, length:]
    imag = spectrum[:, :length] * other[:, length:] + spectrum[:, length:] * other[:, :length]
    high_ref[...], low_ref[...] = split(jnp.concatenate([real, imag], axis=1))
    mixed = three_pass(high_ref, low_ref, inverse)
    twist_cos, twist_sin = twist[0], twist[1]

    def turned(channel):
        part = mixed[channel * groups : (channel + 1) * groups]
        real, imag = part[:, :length], part[:, length:]
        return jnp.concatenate(
            [real * twist_cos - imag * twist_sin, imag * twist_cos + real * twist_sin], axis=0
        )

    for pair in range(CHANNELS // 2):
        high, low = split(jnp.concatenate([turned(2 * pair), turned(2 * pair + 1)], axis=1))
        signal = dot(back[...], jnp.concatenate([high, low, high], axis=0))
        store(2 * pair, signal[:, :length])
        store(2 * pair + 1, signal[:, length:])


def allowed_keys(key_blocks, source, offset, length):
    listed = jnp.max((key_blocks == source).astype(jnp.float32), axis=1, keepdims=True)
    listed = jnp.where(source >= 0, listed, 0.0) > 0.5
    if offset:
        return jnp.broadcast_to(listed, (length, length))
    rows = lax.broadcasted_iota(jnp.int32, (length, length), 0)
    cols = lax.broadcasted_iota(jnp.int32, (length, length), 1)
    return jnp.broadcast_to(listed, (length, length)) & (cols <= rows)


MESH = pl.DeviceIdType.MESH
X, Y, CORES = 4, 8, 2
GROUPS = X * Y * CORES


def terms(me):
    core = lax.rem(me, CORES)
    return lax.div(me, Y * CORES), lax.rem(lax.div(me, CORES), Y), [core, 1 - core]


def for_others(parts, act):
    x, y, cores = parts
    columns = [lax.rem(x + i, X) * (Y * CORES) for i in (2, 1, 3, 0)]

    def row(i, carry):
        half, odd = lax.div(i + 1, 2), lax.rem(i, 2)
        near = lax.rem(y + Y // 2 + half * (1 - 2 * odd), Y) * CORES
        for column in columns:
            for c in range(CORES):
                act(column + near + cores[c])
        return carry

    lax.fori_loop(0, Y - 1, row, 0)
    for column in columns[:-1]:
        for c in range(CORES):
            act(column + y * CORES + cores[c])
    act(columns[-1] + y * CORES + cores[1])


COLUMNS = (1, 2, 3, 0)


def by_column(parts, act):
    x, y, cores = parts

    def rows(column, least):
        for far in range(Y // 2, 0, -1):
            for d in dict.fromkeys((far, Y - far)):
                for c in range(CORES):
                    act(column + lax.rem(y + d, Y) * CORES + cores[c])
        for c in range(least, CORES):
            act(column + y * CORES + cores[c])

    def other(i, carry):
        rows(lax.rem(x + 1 + i, X) * (Y * CORES), 0)
        return carry

    lax.fori_loop(0, X - 1, other, 0)
    rows(x * (Y * CORES), 1)


def rows_of(device):
    return pl.ds(pl.multiple_of(device * CHANNELS, CHANNELS), CHANNELS)


def to_all(source, target, me, parts, send_sem, recv_sem, least=0, others=for_others):
    mine = rows_of(me)

    def send(peer):
        @pl.when(peer >= least)
        def _():
            start_to(source.at[rows_of(peer), :], target.at[mine, :], peer, send_sem, recv_sem)

    others(parts, send)
    pltpu.make_async_copy(source.at[mine, :], target.at[mine, :], recv_sem).start()


def done(ref, sem):
    pltpu.make_async_copy(ref, ref, sem).wait()


def start_to(source, target, peer, send_sem, recv_sem):
    pltpu.make_async_remote_copy(
        src_ref=source,
        dst_ref=target,
        send_sem=send_sem,
        recv_sem=recv_sem,
        device_id={"seq": peer},
        device_id_type=MESH,
    ).start()


def kernel(
    query_hbm, key_hbm, value_hbm, filter_hbm, queries_hbm, keys_hbm, key_blocks_hbm,
    ahead_hbm, back_hbm, twist_hbm, forward_hbm, inverse_hbm,
    hyena, attended,
    gate, gate_key, gate_value, taps, queries, keys, key_blocks, ahead, back, twist, forward, inverse,
    got_taps, got_gate, convolved, got_back, values, high, low, spectrum, weight_high, weight_low,
    here_sem, load_sem, all_send, taps_sem, gate_sem, back_sem, key_send, key_recv, value_send, value_recv,
):
    groups, length = twist.shape[1:]
    span = keys.shape[0]
    heads = queries.shape[1] // HEAD_DIM
    me = lax.axis_index("seq")
    parts = terms(me)
    core = parts[2][0]
    barrier = pltpu.get_barrier_semaphore()

    def greet(peer):
        pl.semaphore_signal(barrier, inc=1, device_id={"seq": peer}, device_id_type=MESH)

    @pl.when(me > 0)
    def _():
        for_others(parts, greet)

    sources = [
        filter_hbm, key_hbm, value_hbm, ahead_hbm, twist_hbm, forward_hbm,
        keys_hbm, back_hbm, inverse_hbm, query_hbm, queries_hbm, key_blocks_hbm,
    ]
    targets = [
        taps, gate_key, gate_value, ahead, twist, forward,
        keys.at[0], back, inverse, gate, queries, key_blocks,
    ]
    loads = [
        pltpu.make_async_copy(source, target, load_sem.at[i])
        for i, (source, target) in enumerate(zip(sources, targets))
    ]
    for load in loads:
        load.start()
    @pl.when(me == 0)
    def _():
        pl.semaphore_wait(barrier, GROUPS - 1)
        for_others(
            parts,
            lambda peer: pl.semaphore_signal(
                here_sem, inc=1, device_id={"seq": peer}, device_id_type=MESH
            ),
        )

    loads[1].wait()
    loads[2].wait()
    gate_key[...] = gate_key[...] * gate_value[...]
    loads[0].wait()

    @pl.when(me > 0)
    def _():
        pl.semaphore_wait(barrier, GROUPS - 2)

    to_all(taps, got_taps, me, parts, all_send.at[0], taps_sem, 1)
    to_all(gate_key, got_gate, me, parts, all_send.at[1], gate_sem, 1)

    @pl.when(me > 0)
    def _():
        pl.semaphore_wait(here_sem, 1)
        mine = rows_of(me)
        start_to(taps.at[rows_of(0), :], got_taps.at[mine, :], 0, all_send.at[0], taps_sem)
        start_to(gate_key.at[rows_of(0), :], got_gate.at[mine, :], 0, all_send.at[1], gate_sem)

    for load in loads[3:]:
        load.wait()

    for o in range(1, span):

        @pl.when(me < o)
        def _():
            keys[o] = jnp.zeros(keys.shape[1:], jnp.float32)
            values[o] = jnp.zeros(values.shape[1:], jnp.float32)

    def block(ref):
        return lambda k: ref[pl.ds(k, groups, stride=CHANNELS), :]

    def store(k, value):
        convolved[pl.ds(k, groups, stride=CHANNELS), :] = value

    def pass_on(own, slots, send_sems, recv_sems):
        @pl.when(me < GROUPS - 2)
        def _():
            start_to(own, slots[2], me + 2, send_sems[2], recv_sems[2])

        @pl.when(core == 0)
        def _():
            start_to(own, slots[1], me + 1, send_sems[1], recv_sems[1])

    def relay(slots, send_sems, recv_sems):
        @pl.when(me >= 2)
        def _():
            done(slots[2], recv_sems[2])

            @pl.when(core == 1)
            def _():
                start_to(slots[2], slots[1], me - 1, send_sems[1], recv_sems[1])

            @pl.when(me < GROUPS - 1)
            def _():
                start_to(slots[2], slots[3], me + 1, send_sems[3], recv_sems[3])

    def arrived(slots, recv_sems):
        @pl.when(me >= 1)
        def _():
            done(slots[1], recv_sems[1])

        @pl.when(me >= 3)
        def _():
            done(slots[3], recv_sems[3])

    def left(slots, send_sems):
        @pl.when(me < GROUPS - 2)
        def _():
            done(slots[2], send_sems[2])

        @pl.when(me != 1)
        def _():
            done(slots[1], send_sems[1])

        @pl.when((me >= 2) & (me < GROUPS - 1))
        def _():
            done(slots[3], send_sems[3])

    key_slots = [keys.at[o] for o in range(span)]
    key_sends = [key_send.at[o] for o in range(span)]
    key_recvs = [key_recv.at[o] for o in range(span)]
    pass_on(key_slots[0], key_slots, key_sends, key_recvs)
    done(got_taps, taps_sem)
    spectrum[...] = to_spectrum(block(got_taps), ahead, twist, forward, high, low)
    done(got_gate, gate_sem)

    signal = to_spectrum(block(got_gate), ahead, twist, forward, high, low)
    multiply_back(signal, spectrum[...], back, twist, inverse, high, low, store)
    to_all(convolved, got_back, me, parts, all_send.at[2], back_sem.at[parts[0]], 0, by_column)
    relay(key_slots, key_sends, key_recvs)

    def in_turn(device):
        x = lax.div(device, Y * CORES)
        return [lax.rem(x + X - turn, X) for turn in COLUMNS]

    def part(head):
        rows = pl.ds(pl.multiple_of(head * HEAD_DIM, HEAD_DIM), HEAD_DIM)
        slots = [hyena.at[rows, :]] + [values.at[o, rows, :] for o in range(1, span)]
        sends = [value_send.at[o, head] for o in range(span)]
        recvs = [value_recv.at[o, head] for o in range(span)]
        return rows, slots, sends, recvs

    for head in in_turn(me):
        rows, slots, sends, recvs = part(head)
        done(got_back.at[rows, :], back_sem.at[head])
        hyena[rows, :] = gate[rows, :] * got_back[rows, :]
        pass_on(slots[0], slots, sends, recvs)

    allowed = [allowed_keys(key_blocks[...], me - o, o, length) for o in range(span)]
    arrived(key_slots, key_recvs)
    for head in in_turn(lax.rem(me + GROUPS - 2, GROUPS)):
        rows, slots, sends, recvs = part(head)
        query = queries[:, rows] * HEAD_DIM ** (-0.5)
        scores = [
            jnp.where(allowed[o], dot_nt(query, keys[o, :, rows], EXACT), -1e30) for o in range(span)
        ]
        top = jnp.max(functools.reduce(jnp.maximum, scores), axis=1, keepdims=True)
        expo = [jnp.exp(s - top) for s in scores]
        total = jnp.sum(functools.reduce(jnp.add, expo), axis=1, keepdims=True)
        weight_high[head], weight_low[head] = split(jnp.concatenate(expo, axis=1) / total)
        relay(slots, sends, recvs)

    for head in in_turn(lax.rem(me + GROUPS - 3, GROUPS)):
        rows, slots, sends, recvs = part(head)
        arrived(slots, recvs)
        value_high, value_low = split(jnp.concatenate([slot[...] for slot in slots], axis=1))
        attended[:, rows] = (
            dot_nt(weight_high[head], value_high)
            + dot_nt(weight_low[head], value_high)
            + dot_nt(weight_high[head], value_low)
        )

    others = (GROUPS - 1) * CHANNELS
    for i, source in enumerate((taps, gate_key, convolved)):
        done(source.at[pl.ds(0, others), :], all_send.at[i])
    left(key_slots, key_sends)
    for head in range(heads):
        rows, slots, sends, recvs = part(head)
        left(slots, sends)


def write_kernel(hyena, attended, hyena_hbm, attended_hbm, sem):
    copies = [
        pltpu.make_async_copy(hyena, hyena_hbm, sem.at[0]),
        pltpu.make_async_copy(attended, attended_hbm, sem.at[1]),
    ]
    for copy in copies:
        copy.start()
    for copy in copies:
        copy.wait()


def body(hyena_query, hyena_key, hyena_value, long_filter, queries, keys, key_blocks):
    channels, length = hyena_key.shape
    groups = lax.axis_size("seq")
    span = key_blocks.shape[1]
    heads = queries.shape[1] // HEAD_DIM
    tables = [jnp.asarray(t) for t in transform_tables(groups, length)]
    square = pltpu.VMEM((channels, length), jnp.float32)
    dma = pltpu.SemaphoreType.DMA
    rows = CHANNELS * groups
    operands = (hyena_query, hyena_key, hyena_value, long_filter, queries, keys, key_blocks, *tables)
    results = pl.pallas_call(
        kernel,
        out_shape=(
            pltpu.VMEM(hyena_query.shape, jnp.float32),
            pltpu.VMEM(queries.shape, jnp.float32),
        ),
        in_specs=[pl.BlockSpec(memory_space=pltpu.HBM)] * len(operands),
        out_specs=(pl.BlockSpec(memory_space=pltpu.VMEM), pl.BlockSpec(memory_space=pltpu.VMEM)),
        scratch_shapes=[
            square,
            square,
            square,
            square,
            pltpu.VMEM(queries.shape, jnp.float32),
            pltpu.VMEM((span, *keys.shape), jnp.float32),
            pltpu.VMEM(key_blocks.shape, jnp.int32),
            *[pltpu.VMEM(t.shape, t.dtype) for t in tables],
            square,
            square,
            square,
            square,
            pltpu.VMEM((span, channels, length), jnp.float32),
            pltpu.VMEM((rows, 2 * length), jnp.bfloat16),
            pltpu.VMEM((rows, 2 * length), jnp.bfloat16),
            pltpu.VMEM((rows, 2 * length), jnp.float32),
            pltpu.VMEM((heads, length, span * length), jnp.bfloat16),
            pltpu.VMEM((heads, length, span * length), jnp.bfloat16),
            pltpu.SemaphoreType.REGULAR,
            dma((len(operands),)),
            dma((3,)),
            dma,
            dma,
            dma((heads,)),
            dma((span,)),
            dma((span,)),
            dma((span, heads)),
            dma((span, heads)),
        ],
        compiler_params=pltpu.CompilerParams(collective_id=0, has_side_effects=True),
    )(*operands)
    return pl.pallas_call(
        write_kernel,
        out_shape=tuple(jax.ShapeDtypeStruct(r.shape, r.dtype) for r in results),
        in_specs=[pl.BlockSpec(memory_space=pl.ANY)] * 2,
        out_specs=[pl.BlockSpec(memory_space=pltpu.HBM)] * 2,
        scratch_shapes=[dma((2,))],
        compiler_params=pltpu.CompilerParams(vmem_limit_bytes=1 << 20),
    )(*results)


def solution(mesh):
    placed = (
        P("chan", "seq"),
        P("chan", "seq"),
        P("chan", "seq"),
        P("chan", "seq"),
        P("seq", "chan"),
        P("seq", "chan"),
        P("seq", None),
    )
    return jax.shard_map(
        body,
        mesh=mesh,
        in_specs=placed,
        out_specs=(P("chan", "seq"), P("seq", "chan")),
        check_vma=False,
    )
```

```python
import functools

import jax
import jax.numpy as jnp
import numpy as np
from jax import lax
from jax.experimental import pallas as pl
from jax.experimental.pallas import tpu as pltpu
from jax.sharding import PartitionSpec as P

HEAD_DIM = 128
EXACT = lax.Precision.HIGHEST
CHANNELS = 8


def split(value):
    high = value.astype(jnp.bfloat16)
    low = (value - high.astype(jnp.float32)).astype(jnp.bfloat16)
    return high, low


def dot(left, right):
    return jnp.dot(left, right, preferred_element_type=jnp.float32)


def dot_nt(left, right, precision=None):
    return lax.dot_general(
        left,
        right,
        (((1,), (1,)), ((), ())),
        precision=precision,
        preferred_element_type=jnp.float32,
    )


def split_table(table):
    high = table.astype(np.float32).astype(jnp.bfloat16)
    low = (table - high.astype(np.float64)).astype(np.float32).astype(jnp.bfloat16)
    return high, low


def transform_tables(groups, length):
    total = 2 * groups * length
    half = np.arange(groups)[:, None] + 0.5
    first = 2 * np.pi * half * np.arange(groups)[None, :] / (2 * groups)
    twist = 2 * np.pi * half * np.arange(length)[None, :] / total
    last = 2 * np.pi * np.arange(length)[:, None] * np.arange(length)[None, :] / length
    ahead = np.concatenate([np.cos(first), -np.sin(first)], axis=0)
    back = ahead.T * (2.0 / total)
    ahead_high, ahead_low = split_table(ahead)
    back_high, back_low = split_table(back)
    cosine, sine = np.cos(last), np.sin(last)
    forward = np.block([[cosine, -sine], [sine, cosine]])
    inverse = np.block([[cosine, sine], [-sine, cosine]])
    return (
        np.concatenate([ahead_high, ahead_high, ahead_low], axis=1),
        np.concatenate([back_high, back_high, back_low], axis=1),
        np.stack([np.cos(twist), np.sin(twist)]).astype(np.float32),
        np.stack(split_table(forward)),
        np.stack(split_table(inverse)),
    )


def three_pass(high_ref, low_ref, table_ref):
    high = high_ref[...]
    return dot(high, table_ref[0]) + dot(low_ref[...], table_ref[0]) + dot(high, table_ref[1])


def to_spectrum(block, ahead, twist, forward, high_ref, low_ref):
    groups, length = twist.shape[1:]
    twist_cos, twist_sin = twist[0], twist[1]
    for pair in range(CHANNELS // 2):
        high, low = split(jnp.concatenate([block(2 * pair), block(2 * pair + 1)], axis=1))
        mixed = dot(ahead[...], jnp.concatenate([high, low, high], axis=0))
        for side in range(2):
            real = mixed[:groups, side * length : (side + 1) * length]
            imag = mixed[groups:, side * length : (side + 1) * length]
            turned = jnp.concatenate(
                [real * twist_cos + imag * twist_sin, imag * twist_cos - real * twist_sin], axis=1
            )
            high, low = split(turned)
            rows = pl.ds((2 * pair + side) * groups, groups)
            high_ref[rows, :] = high
            low_ref[rows, :] = low
    return three_pass(high_ref, low_ref, forward)


def multiply_back(spectrum, other, back, twist, inverse, high_ref, low_ref, store):
    groups, length = twist.shape[1:]
    real = spectrum[:, :length] * other[:, :length] - spectrum[:, length:] * other[:, length:]
    imag = spectrum[:, :length] * other[:, length:] + spectrum[:, length:] * other[:, :length]
    high_ref[...], low_ref[...] = split(jnp.concatenate([real, imag], axis=1))
    mixed = three_pass(high_ref, low_ref, inverse)
    twist_cos, twist_sin = twist[0], twist[1]

    def turned(channel):
        part = mixed[channel * groups : (channel + 1) * groups]
        real, imag = part[:, :length], part[:, length:]
        return jnp.concatenate(
            [real * twist_cos - imag * twist_sin, imag * twist_cos + real * twist_sin], axis=0
        )

    for pair in range(CHANNELS // 2):
        high, low = split(jnp.concatenate([turned(2 * pair), turned(2 * pair + 1)], axis=1))
        signal = dot(back[...], jnp.concatenate([high, low, high], axis=0))
        store(2 * pair, signal[:, :length])
        store(2 * pair + 1, signal[:, length:])


def allowed_keys(key_blocks, source, offset, length):
    listed = jnp.max((key_blocks == source).astype(jnp.float32), axis=1, keepdims=True)
    listed = jnp.where(source >= 0, listed, 0.0) > 0.5
    if offset:
        return jnp.broadcast_to(listed, (length, length))
    rows = lax.broadcasted_iota(jnp.int32, (length, length), 0)
    cols = lax.broadcasted_iota(jnp.int32, (length, length), 1)
    return jnp.broadcast_to(listed, (length, length)) & (cols <= rows)


MESH = pl.DeviceIdType.MESH
X, Y, CORES = 4, 8, 2
GROUPS = X * Y * CORES


def terms(me):
    core = lax.rem(me, CORES)
    return lax.div(me, Y * CORES), lax.rem(lax.div(me, CORES), Y), [core, 1 - core]


def for_others(parts, act):
    x, y, cores = parts
    columns = [lax.rem(x + i, X) * (Y * CORES) for i in (2, 1, 3, 0)]

    def row(i, carry):
        half, odd = lax.div(i + 1, 2), lax.rem(i, 2)
        near = lax.rem(y + Y // 2 + half * (1 - 2 * odd), Y) * CORES
        for column in columns:
            for c in range(CORES):
                act(column + near + cores[c])
        return carry

    lax.fori_loop(0, Y - 1, row, 0)
    for column in columns[:-1]:
        for c in range(CORES):
            act(column + y * CORES + cores[c])
    act(columns[-1] + y * CORES + cores[1])


COLUMNS = (1, 2, 3, 0)
WRITES = 4


def by_column(parts, act):
    x, y, cores = parts

    def rows(column, least):
        for far in range(Y // 2, 0, -1):
            for d in dict.fromkeys((far, Y - far)):
                for c in range(CORES):
                    act(column + lax.rem(y + d, Y) * CORES + cores[c])
        for c in range(least, CORES):
            act(column + y * CORES + cores[c])

    def other(i, carry):
        rows(lax.rem(x + 1 + i, X) * (Y * CORES), 0)
        return carry

    lax.fori_loop(0, X - 1, other, 0)
    rows(x * (Y * CORES), 1)


def rows_of(device):
    return pl.ds(pl.multiple_of(device * CHANNELS, CHANNELS), CHANNELS)


def to_all(source, target, me, parts, send_sem, recv_sem, least=0, others=for_others):
    mine = rows_of(me)

    def send(peer):
        @pl.when(peer >= least)
        def _():
            start_to(source.at[rows_of(peer), :], target.at[mine, :], peer, send_sem, recv_sem)

    others(parts, send)
    pltpu.make_async_copy(source.at[mine, :], target.at[mine, :], recv_sem).start()


def done(ref, sem):
    pltpu.make_async_copy(ref, ref, sem).wait()


def start_to(source, target, peer, send_sem, recv_sem):
    pltpu.make_async_remote_copy(
        src_ref=source,
        dst_ref=target,
        send_sem=send_sem,
        recv_sem=recv_sem,
        device_id={"seq": peer},
        device_id_type=MESH,
    ).start()


def kernel(
    query_hbm, key_hbm, value_hbm, filter_hbm, queries_hbm, keys_hbm, key_blocks_hbm,
    ahead_hbm, back_hbm, twist_hbm, forward_hbm, inverse_hbm,
    hyena, attended,
    gate, gate_key, gate_value, taps, queries, keys, key_blocks, ahead, back, twist, forward, inverse,
    got_taps, got_gate, convolved, got_back, values, high, low, spectrum, weight_high, weight_low,
    here_sem, load_sem, all_send, taps_sem, gate_sem, back_sem, key_send, key_recv, value_send, value_recv,
):
    groups, length = twist.shape[1:]
    span = keys.shape[0]
    heads = queries.shape[1] // HEAD_DIM
    me = lax.axis_index("seq")
    parts = terms(me)
    core = parts[2][0]
    barrier = pltpu.get_barrier_semaphore()

    def greet(peer):
        pl.semaphore_signal(barrier, inc=1, device_id={"seq": peer}, device_id_type=MESH)

    @pl.when(me > 0)
    def _():
        for_others(parts, greet)

    sources = [
        filter_hbm, key_hbm, value_hbm, ahead_hbm, twist_hbm, forward_hbm,
        keys_hbm, back_hbm, inverse_hbm, query_hbm, queries_hbm, key_blocks_hbm,
    ]
    targets = [
        taps, gate_key, gate_value, ahead, twist, forward,
        keys.at[0], back, inverse, gate, queries, key_blocks,
    ]
    loads = [
        pltpu.make_async_copy(source, target, load_sem.at[i])
        for i, (source, target) in enumerate(zip(sources, targets))
    ]
    for load in loads:
        load.start()
    @pl.when(me == 0)
    def _():
        pl.semaphore_wait(barrier, GROUPS - 1)
        for_others(
            parts,
            lambda peer: pl.semaphore_signal(
                here_sem, inc=1, device_id={"seq": peer}, device_id_type=MESH
            ),
        )

    loads[1].wait()
    loads[2].wait()
    gate_key[...] = gate_key[...] * gate_value[...]
    loads[0].wait()

    @pl.when(me > 0)
    def _():
        pl.semaphore_wait(barrier, GROUPS - 2)

    to_all(taps, got_taps, me, parts, all_send.at[0], taps_sem, 1)
    to_all(gate_key, got_gate, me, parts, all_send.at[1], gate_sem, 1)

    @pl.when(me > 0)
    def _():
        pl.semaphore_wait(here_sem, 1)
        mine = rows_of(me)
        start_to(taps.at[rows_of(0), :], got_taps.at[mine, :], 0, all_send.at[0], taps_sem)
        start_to(gate_key.at[rows_of(0), :], got_gate.at[mine, :], 0, all_send.at[1], gate_sem)

    for load in loads[3:]:
        load.wait()

    for o in range(1, span):

        @pl.when(me < o)
        def _():
            keys[o] = jnp.zeros(keys.shape[1:], jnp.float32)
            values[o] = jnp.zeros(values.shape[1:], jnp.float32)

    def block(ref):
        return lambda k: ref[pl.ds(k, groups, stride=CHANNELS), :]

    def store(k, value):
        convolved[pl.ds(k, groups, stride=CHANNELS), :] = value

    def pass_on(own, slots, send_sems, recv_sems):
        @pl.when(me < GROUPS - 2)
        def _():
            start_to(own, slots[2], me + 2, send_sems[2], recv_sems[2])

        @pl.when(core == 0)
        def _():
            start_to(own, slots[1], me + 1, send_sems[1], recv_sems[1])

    def relay(slots, send_sems, recv_sems):
        @pl.when(me >= 2)
        def _():
            done(slots[2], recv_sems[2])

            @pl.when(core == 1)
            def _():
                start_to(slots[2], slots[1], me - 1, send_sems[1], recv_sems[1])

            @pl.when(me < GROUPS - 1)
            def _():
                start_to(slots[2], slots[3], me + 1, send_sems[3], recv_sems[3])

    def arrived(slots, recv_sems):
        @pl.when(me >= 1)
        def _():
            done(slots[1], recv_sems[1])

        @pl.when(me >= 3)
        def _():
            done(slots[3], recv_sems[3])

    def left(slots, send_sems):
        @pl.when(me < GROUPS - 2)
        def _():
            done(slots[2], send_sems[2])

        @pl.when(me != 1)
        def _():
            done(slots[1], send_sems[1])

        @pl.when((me >= 2) & (me < GROUPS - 1))
        def _():
            done(slots[3], send_sems[3])

    key_slots = [keys.at[o] for o in range(span)]
    key_sends = [key_send.at[o] for o in range(span)]
    key_recvs = [key_recv.at[o] for o in range(span)]
    pass_on(key_slots[0], key_slots, key_sends, key_recvs)
    done(got_taps, taps_sem)
    spectrum[...] = to_spectrum(block(got_taps), ahead, twist, forward, high, low)
    done(got_gate, gate_sem)

    signal = to_spectrum(block(got_gate), ahead, twist, forward, high, low)
    multiply_back(signal, spectrum[...], back, twist, inverse, high, low, store)
    to_all(convolved, got_back, me, parts, all_send.at[2], back_sem.at[parts[0]], 0, by_column)
    relay(key_slots, key_sends, key_recvs)

    def in_turn(device):
        x = lax.div(device, Y * CORES)
        return [lax.rem(x + X - turn, X) for turn in COLUMNS]

    def part(head):
        rows = pl.ds(pl.multiple_of(head * HEAD_DIM, HEAD_DIM), HEAD_DIM)
        slots = [hyena.at[rows, :]] + [values.at[o, rows, :] for o in range(1, span)]
        sends = [value_send.at[o, head] for o in range(span)]
        recvs = [value_recv.at[o, head] for o in range(span)]
        return rows, slots, sends, recvs

    for head in in_turn(me):
        rows, slots, sends, recvs = part(head)
        done(got_back.at[rows, :], back_sem.at[head])
        hyena[rows, :] = gate[rows, :] * got_back[rows, :]
        pass_on(slots[0], slots, sends, recvs)

    allowed = [allowed_keys(key_blocks[...], me - o, o, length) for o in range(span)]
    arrived(key_slots, key_recvs)
    for head in in_turn(lax.rem(me + GROUPS - 2, GROUPS)):
        rows, slots, sends, recvs = part(head)
        query = queries[:, rows] * HEAD_DIM ** (-0.5)
        scores = [
            jnp.where(allowed[o], dot_nt(query, keys[o, :, rows], EXACT), -1e30) for o in range(span)
        ]
        top = jnp.max(functools.reduce(jnp.maximum, scores), axis=1, keepdims=True)
        expo = [jnp.exp(s - top) for s in scores]
        total = jnp.sum(functools.reduce(jnp.add, expo), axis=1, keepdims=True)
        weight_high[head], weight_low[head] = split(jnp.concatenate(expo, axis=1) / total)
        relay(slots, sends, recvs)

    for head in in_turn(lax.rem(me + GROUPS - 3, GROUPS)):
        rows, slots, sends, recvs = part(head)
        arrived(slots, recvs)
        value_high, value_low = split(jnp.concatenate([slot[...] for slot in slots], axis=1))
        attended[:, rows] = (
            dot_nt(weight_high[head], value_high)
            + dot_nt(weight_low[head], value_high)
            + dot_nt(weight_high[head], value_low)
        )

    others = (GROUPS - 1) * CHANNELS
    for i, source in enumerate((taps, gate_key, convolved)):
        done(source.at[pl.ds(0, others), :], all_send.at[i])
    left(key_slots, key_sends)
    for head in range(heads):
        rows, slots, sends, recvs = part(head)
        left(slots, sends)


def write_kernel(hyena, attended, hyena_hbm, attended_hbm, sem):
    copies = []
    for source, target in ((attended, attended_hbm), (hyena, hyena_hbm)):
        size = source.shape[0] // WRITES
        for i in range(WRITES):
            rows = pl.ds(i * size, size)
            copies.append(
                pltpu.make_async_copy(source.at[rows, :], target.at[rows, :], sem.at[len(copies)])
            )
    for copy in copies:
        copy.start()
    for copy in copies:
        copy.wait()


def body(hyena_query, hyena_key, hyena_value, long_filter, queries, keys, key_blocks):
    channels, length = hyena_key.shape
    groups = lax.axis_size("seq")
    span = key_blocks.shape[1]
    heads = queries.shape[1] // HEAD_DIM
    tables = [jnp.asarray(t) for t in transform_tables(groups, length)]
    square = pltpu.VMEM((channels, length), jnp.float32)
    dma = pltpu.SemaphoreType.DMA
    rows = CHANNELS * groups
    operands = (hyena_query, hyena_key, hyena_value, long_filter, queries, keys, key_blocks, *tables)
    results = pl.pallas_call(
        kernel,
        out_shape=(
            pltpu.VMEM(hyena_query.shape, jnp.float32),
            pltpu.VMEM(queries.shape, jnp.float32),
        ),
        in_specs=[pl.BlockSpec(memory_space=pltpu.HBM)] * len(operands),
        out_specs=(pl.BlockSpec(memory_space=pltpu.VMEM), pl.BlockSpec(memory_space=pltpu.VMEM)),
        scratch_shapes=[
            square,
            square,
            square,
            square,
            pltpu.VMEM(queries.shape, jnp.float32),
            pltpu.VMEM((span, *keys.shape), jnp.float32),
            pltpu.VMEM(key_blocks.shape, jnp.int32),
            *[pltpu.VMEM(t.shape, t.dtype) for t in tables],
            square,
            square,
            square,
            square,
            pltpu.VMEM((span, channels, length), jnp.float32),
            pltpu.VMEM((rows, 2 * length), jnp.bfloat16),
            pltpu.VMEM((rows, 2 * length), jnp.bfloat16),
            pltpu.VMEM((rows, 2 * length), jnp.float32),
            pltpu.VMEM((heads, length, span * length), jnp.bfloat16),
            pltpu.VMEM((heads, length, span * length), jnp.bfloat16),
            pltpu.SemaphoreType.REGULAR,
            dma((len(operands),)),
            dma((3,)),
            dma,
            dma,
            dma((heads,)),
            dma((span,)),
            dma((span,)),
            dma((span, heads)),
            dma((span, heads)),
        ],
        compiler_params=pltpu.CompilerParams(collective_id=0, has_side_effects=True),
    )(*operands)
    return pl.pallas_call(
        write_kernel,
        out_shape=tuple(jax.ShapeDtypeStruct(r.shape, r.dtype) for r in results),
        in_specs=[pl.BlockSpec(memory_space=pl.ANY)] * 2,
        out_specs=[pl.BlockSpec(memory_space=pltpu.HBM)] * 2,
        scratch_shapes=[dma((2 * WRITES,))],
        compiler_params=pltpu.CompilerParams(vmem_limit_bytes=1 << 20),
    )(*results)


def solution(mesh):
    placed = (
        P("chan", "seq"),
        P("chan", "seq"),
        P("chan", "seq"),
        P("chan", "seq"),
        P("seq", "chan"),
        P("seq", "chan"),
        P("seq", None),
    )
    return jax.shard_map(
        body,
        mesh=mesh,
        in_specs=placed,
        out_specs=(P("chan", "seq"), P("seq", "chan")),
        check_vma=False,
    )
```
